32 devices in a mesh: blk: 8 (over z, x), grp: 4 (over y, core).
Axes of the slice: x: 2, y: 2, z: 4, core: 2. Of those that a mesh axis runs over, the one named last changes fastest.
Arguments:
- tokens: bfloat16 [512, 8192], P(('blk', 'grp')), may hold values from -6 to 6
- cotangent: bfloat16 [512, 8192], P(('blk', 'grp')), may hold values from -6 to 6
- gate_weight: bfloat16 [8192, 4096], P(None, 'blk'), may hold values from -0.0625 to 0.0625
- up_weight: bfloat16 [8192, 4096], P(None, 'blk'), may hold values from -0.0625 to 0.0625
- down_weight: bfloat16 [4096, 8192], P('blk'), may hold values from -0.09375 to 0.09375
- a_gate: bfloat16 [256, 16, 8192], P('blk'), may hold values from -0.0625 to 0.0625
- a_up: bfloat16 [256, 16, 8192], P('blk'), may hold values from -0.0625 to 0.0625
- down_output_factors: bfloat16 [256, 16, 8192], P('blk'), may hold values from -0.375 to 0.375
- b_gate: bfloat16 [256, 16, 4096], P(None, None, 'blk'), may hold values from -0.375 to 0.375
- b_up: bfloat16 [256, 16, 4096], P(None, None, 'blk'), may hold values from -0.375 to 0.375
- a_down: bfloat16 [256, 16, 4096], P(None, None, 'blk'), may hold values from -0.09375 to 0.09375
- tenant_of_row: int32 [512], replicated, may hold values from 0 to 255, as said below
- adapter_slot: int32 [256], replicated, may hold values from 0 to 255, as said below
Outputs:
- mixed: bfloat16 [512, 8192], P(('blk', 'grp'))
- input_grad: bfloat16 [512, 8192], P(('blk', 'grp'))
- grad_a_gate: float32 [256, 16, 8192], P(('blk', 'grp'))
- grad_a_up: float32 [256, 16, 8192], P(('blk', 'grp'))
- grad_b_down: float32 [256, 16, 8192], P(('blk', 'grp'))
- grad_b_gate: float32 [256, 16, 4096], P('grp', None, 'blk')
- grad_b_up: float32 [256, 16, 4096], P('grp', None, 'blk')
- grad_a_down: float32 [256, 16, 4096], P('grp', None, 'blk')
The draws below stay inside these ranges and needn't reach their ends.
Inputs may be any that keep to these rules, and one draw needn't show every extreme that they name: `tenant_of_row`: among the rows held by the devices of one index of grp, for each index b of blk at most 32 rows have tenants whose adapter slot s has s // 32 == b, and for some b exactly 32 do. A permutation: tenant t's factors in a_gate, a_up and down_output_factors, and its gradients of them, stand at index adapter_slot[t].
All inputs are finite; a program needn't handle non-finite values.
Results may differ from the reference program's by a relative error of at most 0.02.
Values may be sent and summed in bfloat16 or wider, within the bound.
A program may use at most 192 MiB of HBM per device.

```python
import jax
import jax.numpy as jnp
from jax import lax

D = 8192
FF = 4096
RANK = 16
TENANTS = 256
TOK_DEV = 16
TOKENS = 512
GROUP_ROWS = 128
N_BLK = 8


def tenant_layout(key):
    base_key = jax.random.fold_in(key, 7013)
    slot_perm = jax.random.permutation(jax.random.fold_in(base_key, 1), TENANTS).astype(jnp.int32)
    tenant_at = jnp.argsort(slot_perm, stable=True).astype(jnp.int32)
    blocks = GROUP_ROWS // TOK_DEV
    groups = TOKENS // GROUP_ROWS
    per_owner = TENANTS // blocks
    capacity = 2 * TOK_DEV

    def one_group(group_key):
        sub_keys = jax.random.split(group_key, 4)
        owner_sorting = jax.random.permutation(sub_keys[0], blocks).astype(jnp.int32)
        pair_split = jax.random.randint(sub_keys[1], (blocks // 2,), 0, capacity + 1).astype(jnp.int32)
        pair_split = pair_split.at[0].set(0)
        owner_loads = jnp.zeros((blocks,), jnp.int32).at[owner_sorting[0::2]].set(pair_split)
        owner_loads = owner_loads.at[owner_sorting[1::2]].set(capacity - pair_split)
        bounds = jnp.cumsum(owner_loads).astype(jnp.int32)
        row_owner = jnp.searchsorted(bounds, jnp.arange(GROUP_ROWS, dtype=jnp.int32), side='right').astype(jnp.int32)
        row_owner = row_owner[jax.random.permutation(sub_keys[2], GROUP_ROWS)]
        local_pick = jax.random.randint(sub_keys[3], (GROUP_ROWS,), 0, per_owner).astype(jnp.int32)
        return tenant_at[row_owner * per_owner + local_pick]
    group_keys = jax.random.split(jax.random.fold_in(base_key, 2), groups)
    layout_rows = jax.vmap(one_group)(group_keys)
    layout_rows = layout_rows.reshape(groups, blocks, TOK_DEV).transpose(1, 0, 2).reshape(TOKENS)
    return (layout_rows.astype(jnp.int32), slot_perm)


def draw_tenant_of_row(key, part):
    return tenant_layout(key)[0]


def draw_adapter_slot(key, part):
    return tenant_layout(key)[1]


def block_levels(stream_key, extent, pieces, least, high):
    level, own = 1.0, jax.random.fold_in(stream_key, 6)
    for axis_at, blocks in pieces:
        draws = jnp.exp(jax.random.uniform(jax.random.fold_in(own, axis_at), (blocks,), jnp.float32, least / len(pieces), high / len(pieces)))
        level = level * jnp.repeat(draws, extent[axis_at] // blocks).reshape([-1 if axis == axis_at else 1 for axis in range(len(extent))])
    return level


def centred(rng, extent, width, most, shards=(), kind=jnp.bfloat16):
    loudness = block_levels(rng, extent, shards, -0.22, 0.18) if shards else 1.0
    result = jax.random.normal(rng, extent, jnp.float32) * width * loudness
    return jnp.minimum(jnp.maximum(result, -most), most).astype(kind)


def setup_inputs(seed: int = 0) -> dict:
    streams_of = jax.random.split(jax.random.key(seed), 14)
    tokens = centred(streams_of[0], (TOKENS, D), 1.0, 6.0, ((0, 32),))
    cotangent = centred(streams_of[1], (TOKENS, D), 0.5, 6.0, ((0, 32),))
    gate_weight = centred(streams_of[2], (D, FF), D ** -0.5, 0.0625, ((1, 8),))
    up_weight = centred(streams_of[3], (D, FF), D ** -0.5, 0.0625, ((1, 8),))
    down_weight = centred(streams_of[4], (FF, D), FF ** -0.5, 0.09375, ((0, 8),))
    a_gate = centred(streams_of[5], (TENANTS, RANK, D), D ** -0.5, 0.0625, ((0, 8),))
    a_up = centred(streams_of[6], (TENANTS, RANK, D), D ** -0.5, 0.0625, ((0, 8),))
    down_output_factors = centred(streams_of[7], (TENANTS, RANK, D), (16 * RANK) ** -0.5, 0.375, ((0, 8),))
    b_gate = centred(streams_of[8], (TENANTS, RANK, FF), (16 * RANK) ** -0.5, 0.375, ((2, 8),))
    b_up = centred(streams_of[9], (TENANTS, RANK, FF), (16 * RANK) ** -0.5, 0.375, ((2, 8),))
    a_down = centred(streams_of[10], (TENANTS, RANK, FF), FF ** -0.5, 0.09375, ((2, 8),))
    tenant_of_row = draw_tenant_of_row(jax.random.fold_in(streams_of[13], 71), 0)
    adapter_slot = draw_adapter_slot(jax.random.fold_in(streams_of[13], 71), 0)
    return {"tokens": tokens, "cotangent": cotangent, "gate_weight": gate_weight, "up_weight": up_weight, "down_weight": down_weight, "a_gate": a_gate, "a_up": a_up, "down_output_factors": down_output_factors, "b_gate": b_gate, "b_up": b_up, "a_down": a_down, "tenant_of_row": tenant_of_row, "adapter_slot": adapter_slot}


adapter_scale = 2.0


def silu_pair(gate_in):
    sigmoid_val = jax.nn.sigmoid(gate_in)
    return gate_in * sigmoid_val, sigmoid_val * (1.0 + gate_in * (1.0 - sigmoid_val))


def contract_dims(left_op, right_op, form):
    return jnp.einsum(form, left_op.astype(jnp.float32), right_op.astype(jnp.float32), precision=lax.Precision.HIGHEST)


def round_sum(parts):
    rounded = lax.optimization_barrier(parts.astype(jnp.bfloat16))
    return jnp.sum(rounded.astype(jnp.float32), axis=1).astype(jnp.bfloat16)


def reference(tokens, cotangent, gate_weight, up_weight, down_weight, a_gate, a_up, down_output_factors, b_gate, b_up, a_down, tenant_of_row, adapter_slot):
    per_owner = TENANTS // N_BLK
    unit_width = FF // N_BLK
    block_rows = 128 if TOKENS % 128 == 0 else TOKENS
    num_blocks = TOKENS // block_rows
    slot_of_row = adapter_slot[tenant_of_row].astype(jnp.int32)
    gate_blocks = gate_weight.reshape(D, N_BLK, unit_width)
    up_blocks = up_weight.reshape(D, N_BLK, unit_width)
    down_blocks = down_weight.reshape(N_BLK, unit_width, D)

    def one_block(totals, block_id):
        first_row = (block_id * block_rows).astype(jnp.int32)
        row_x = lax.dynamic_slice_in_dim(tokens, first_row, block_rows, 0)
        row_dy = lax.dynamic_slice_in_dim(cotangent, first_row, block_rows, 0)
        row_slot = lax.dynamic_slice_in_dim(slot_of_row, first_row, block_rows, 0)
        row_tenant = lax.dynamic_slice_in_dim(tenant_of_row.astype(jnp.int32), first_row, block_rows, 0)
        row_owner = row_slot // per_owner
        fac_ag = a_gate[row_slot]
        fac_au = a_up[row_slot]
        fac_bd = down_output_factors[row_slot]
        fac_bg = b_gate[row_tenant]
        fac_bu = b_up[row_tenant]
        fac_ad = a_down[row_tenant]
        p_gate = contract_dims(row_x, fac_ag, "nd,nrd->nr").astype(jnp.bfloat16)
        p_up = contract_dims(row_x, fac_au, "nd,nrd->nr").astype(jnp.bfloat16)
        grad_q = (adapter_scale * contract_dims(row_dy, fac_bd, "nd,nrd->nr")).astype(jnp.bfloat16)
        gate_val = jnp.dot(row_x, gate_weight, preferred_element_type=jnp.float32) + adapter_scale * contract_dims(p_gate, fac_bg, "nr,nrf->nf")
        up_val = jnp.dot(row_x, up_weight, preferred_element_type=jnp.float32) + adapter_scale * contract_dims(p_up, fac_bu, "nr,nrf->nf")
        act_val, act_slope = silu_pair(gate_val)
        hidden = (act_val * up_val).astype(jnp.bfloat16)
        low_q = contract_dims(hidden, fac_ad, "nf,nrf->nr").astype(jnp.bfloat16)
        owner_hot = (row_owner[:, None] == jnp.arange(N_BLK, dtype=jnp.int32)[None, :]).astype(jnp.float32)
        mixed_extra = adapter_scale * contract_dims(low_q, fac_bd, "nr,nrd->nd")
        mixed_parts = contract_dims(hidden.reshape(block_rows, N_BLK, unit_width), down_blocks, "nkf,kfd->nkd") + owner_hot[:, :, None] * mixed_extra[:, None, :]
        mixed_rows = round_sum(mixed_parts)
        grad_h = lax.dot_general(row_dy, down_weight, (((1,), (1,)), ((), ())), preferred_element_type=jnp.float32) + contract_dims(grad_q, fac_ad, "nr,nrf->nf")
        grad_gate = (grad_h * up_val * act_slope).astype(jnp.bfloat16)
        grad_up = (grad_h * act_val).astype(jnp.bfloat16)
        dp_gate = (adapter_scale * contract_dims(grad_gate, fac_bg, "nf,nrf->nr")).astype(jnp.bfloat16)
        dp_up = (adapter_scale * contract_dims(grad_up, fac_bu, "nf,nrf->nr")).astype(jnp.bfloat16)
        input_extra = contract_dims(dp_gate, fac_ag, "nr,nrd->nd") + contract_dims(dp_up, fac_au, "nr,nrd->nd")
        input_parts = contract_dims(grad_gate.reshape(block_rows, N_BLK, unit_width), gate_blocks, "nkf,dkf->nkd")
        input_parts = input_parts + contract_dims(grad_up.reshape(block_rows, N_BLK, unit_width), up_blocks, "nkf,dkf->nkd")
        input_parts = input_parts + owner_hot[:, :, None] * input_extra[:, None, :]
        input_rows = round_sum(input_parts)
        sum_ag = totals[0] + jax.ops.segment_sum(contract_dims(dp_gate, row_x, "nr,nd->nrd"), row_slot, num_segments=TENANTS)
        sum_au = totals[1] + jax.ops.segment_sum(contract_dims(dp_up, row_x, "nr,nd->nrd"), row_slot, num_segments=TENANTS)
        sum_bd = totals[2] + adapter_scale * jax.ops.segment_sum(contract_dims(low_q, row_dy, "nr,nd->nrd"), row_slot, num_segments=TENANTS)
        sum_bg = totals[3] + adapter_scale * jax.ops.segment_sum(contract_dims(p_gate, grad_gate, "nr,nf->nrf"), row_tenant, num_segments=TENANTS)
        sum_bu = totals[4] + adapter_scale * jax.ops.segment_sum(contract_dims(p_up, grad_up, "nr,nf->nrf"), row_tenant, num_segments=TENANTS)
        sum_ad = totals[5] + jax.ops.segment_sum(contract_dims(grad_q, hidden, "nr,nf->nrf"), row_tenant, num_segments=TENANTS)
        return (sum_ag, sum_au, sum_bd, sum_bg, sum_bu, sum_ad), (mixed_rows, input_rows)

    zeros_d = jnp.zeros((TENANTS, RANK, D), jnp.float32)
    zero_feature_block = jnp.zeros((TENANTS, RANK, FF), jnp.float32)
    totals, stacked = lax.scan(one_block, (zeros_d, zeros_d, zeros_d, zero_feature_block, zero_feature_block, zero_feature_block), jnp.arange(num_blocks, dtype=jnp.int32))
    mixed = stacked[0].reshape(TOKENS, D)
    input_grad = stacked[1].reshape(TOKENS, D)
    return (mixed, input_grad, totals[0], totals[1], totals[2], totals[3], totals[4], totals[5])
```

```python
import functools

import jax
import jax.numpy as jnp
from jax import lax
from jax.experimental import pallas as pl
from jax.experimental.pallas import tpu as pltpu
from jax.sharding import PartitionSpec as P

MESH = pl.DeviceIdType.MESH
bf16 = jnp.bfloat16
f32 = jnp.float32


def remote(src, dst, send, recv, to):
    return pltpu.make_async_remote_copy(
        src_ref=src,
        dst_ref=dst,
        send_sem=send,
        recv_sem=recv,
        device_id={"blk": to},
        device_id_type=MESH,
    )


def place(blocks):
    me = lax.axis_index("blk")
    line = blocks // 2
    row = me // 2
    col = me - 2 * row
    partner = me + 1 - 2 * col
    return me, line, row, col, partner


def greet(me, line, row, partner):
    barrier = pltpu.get_barrier_semaphore()
    pl.semaphore_signal(barrier, inc=1, device_id={"blk": partner}, device_id_type=MESH)

    @pl.when(row < line - 1)
    def _():
        pl.semaphore_signal(barrier, inc=1, device_id={"blk": me + 2}, device_id_type=MESH)

    @pl.when(row > 0)
    def _():
        pl.semaphore_signal(barrier, inc=1, device_id={"blk": me - 2}, device_id_type=MESH)

    peers = 1 + (row < line - 1).astype(jnp.int32) + (row > 0).astype(jnp.int32)
    pl.semaphore_wait(barrier, peers)


def gather_kernel(
    blocks, x_ref, d_ref, xo_ref, do_ref, own_sem, up_s, up_r, dn_s, dn_r, ac_s, ac_r, ex_s, ex_r
):
    me, line, row, col, partner = place(blocks)
    outs = (xo_ref, do_ref)
    ins = (x_ref, d_ref)
    above, below = me + 2, me - 2

    def up_copy(c, src, block, s):
        return remote(src, outs[c].at[block], up_s.at[c, s], up_r.at[c, s], above)

    def dn_copy(c, src, block, s):
        return remote(src, outs[c].at[block], dn_s.at[c, s], dn_r.at[c, s], below)

    def ac_copy(c, src, at):
        return remote(
            src, outs[c].at[2 * at + col], ac_s.at[c, at], ac_r.at[c, at], partner
        )

    def ac_arrival(c, at):
        ref = outs[c].at[2 * at + 1 - col]
        return remote(ref, ref, ac_s.at[c, at], ac_r.at[c, at], partner)

    def ex_copy(direction, to):
        ref = do_ref.at[partner]
        return remote(ref, ref, ex_s.at[direction], ex_r.at[direction], to)

    def ex_arrival(direction, block, to):
        ref = do_ref.at[block]
        return remote(ref, ref, ex_s.at[direction], ex_r.at[direction], to)

    greet(me, line, row, partner)
    own = []
    for c in range(2):
        ac_copy(c, ins[c], row).start()

        @pl.when(row < line - 1)
        def _():
            up_copy(c, ins[c], me, 0).start()

        @pl.when(row > 0)
        def _():
            dn_copy(c, ins[c], me, 0).start()

    for c in range(2):
        copy = pltpu.make_async_copy(ins[c], outs[c].at[me], own_sem.at[c])
        copy.start()
        own.append(copy)
    for s in range(1, line):
        for c in range(2):

            @pl.when(row >= s)
            def _():
                block = me - 2 * s
                ref = outs[c].at[block]
                up_copy(c, ref, block, s - 1).wait_recv()
                if s < line - 1:

                    @pl.when(row < line - 1)
                    def _():
                        up_copy(c, ref, block, s).start()

                if c == 0 or s > 1:
                    ac_copy(c, ref, row - s).start()

            @pl.when(row + s < line)
            def _():
                block = me + 2 * s
                ref = outs[c].at[block]
                dn_copy(c, ref, block, s - 1).wait_recv()
                if s < line - 1:

                    @pl.when(row > 0)
                    def _():
                        dn_copy(c, ref, block, s).start()

                if c == 0 or s > 1:
                    ac_copy(c, ref, row + s).start()

        if s == 1:
            ac_arrival(1, row).wait_recv()

            @pl.when(row < line - 1)
            def _():
                ex_copy(0, above).start()

            @pl.when(row > 0)
            def _():
                ex_copy(1, below).start()

    ac_arrival(0, row).wait_recv()
    ac_copy(0, x_ref, row).wait_send()
    ac_copy(1, d_ref, row).wait_send()
    for s in range(1, line):
        for c in range(2):
            for ok, at in ((row >= s, row - s), (row + s < line, row + s)):

                @pl.when(ok)
                def _():
                    if c == 0 or s > 1:
                        ac_arrival(c, at).wait_recv()
                        ac_copy(c, outs[c].at[2 * at + col], at).wait_send()

    @pl.when(row > 0)
    def _():
        ex_arrival(0, partner - 2, above).wait_recv()
        ex_copy(1, below).wait_send()

    @pl.when(row < line - 1)
    def _():
        ex_arrival(1, partner + 2, below).wait_recv()
        ex_copy(0, above).wait_send()

    for s in range(line - 1):
        for c in range(2):

            @pl.when((row >= s) & (row < line - 1))
            def _():
                src = ins[c] if s == 0 else outs[c].at[me - 2 * s]
                up_copy(c, src, me - 2 * s, s).wait_send()

            @pl.when((row + s < line) & (row > 0))
            def _():
                src = ins[c] if s == 0 else outs[c].at[me + 2 * s]
                dn_copy(c, src, me + 2 * s, s).wait_send()

    for copy in own:
        copy.wait()


def gather_rows(blocks, x, dy):
    line = blocks // 2
    shape = jax.ShapeDtypeStruct((blocks,) + x.shape, x.dtype)
    dma = pltpu.SemaphoreType.DMA
    got = pl.pallas_call(
        functools.partial(gather_kernel, blocks),
        out_shape=(shape, shape),
        in_specs=[pl.BlockSpec(memory_space=pltpu.VMEM)] * 2,
        out_specs=(pl.BlockSpec(memory_space=pl.ANY),) * 2,
        scratch_shapes=[dma((2,))] + [dma((2, line))] * 6 + [dma((2,))] * 2,
        compiler_params=pltpu.CompilerParams(
            collective_id=0, has_side_effects=True, vmem_limit_bytes=4 * 2**20
        ),
        name="gather_rows",
    )(x, dy)
    return [part.reshape((-1,) + x.shape[1:]) for part in got]


def scatter_kernel(
    blocks,
    m_ref,
    b_ref,
    mo_ref,
    bo_ref,
    pair_buf,
    line_buf,
    top_buf,
    ex_buf,
    cross_buf,
    ac_s,
    ac_r,
    up_s,
    up_r,
    dn_s,
    dn_r,
    ex_s,
    ex_r,
):
    me, line, row, col, partner = place(blocks)
    parts = (m_ref, b_ref)
    outs = (mo_ref, bo_ref)
    above, below = me + 2, me - 2
    width = m_ref.shape[-1]
    tile = width // 8

    def total(dst, srcs):
        def body(k, carry):
            at = pl.ds(pl.multiple_of(k * tile, tile), tile)
            acc = srcs[0][:, at].astype(f32)
            for src in srcs[1:]:
                acc = acc + src[:, at].astype(f32)
            dst[:, at] = acc.astype(dst.dtype)
            return carry

        lax.fori_loop(0, width // tile, body, 0)

    def ac_copy(c, src, at):
        return remote(src, pair_buf.at[c, at], ac_s.at[c, at], ac_r.at[c, at], partner)

    def up_copy(c, at):
        return remote(
            pair_buf.at[c, at], line_buf.at[c, at], up_s.at[c, at], up_r.at[c, at], above
        )

    def dn_copy(c, at, landing):
        return remote(pair_buf.at[c, at], landing, dn_s.at[c, at], dn_r.at[c, at], below)

    def ex_copy(direction, block, to):
        return remote(
            b_ref.at[block], ex_buf.at[direction], ex_s.at[direction], ex_r.at[direction], to
        )

    greet(me, line, row, partner)

    @pl.when(row < line - 1)
    def _():
        ex_copy(0, partner + 2, above).start()

    @pl.when(row > 0)
    def _():
        ex_copy(1, partner - 2, below).start()

    def spots(s):
        if s == 0:
            return ((None, row),)
        return ((row + s < line, row + s), (row >= s, row - s))

    def crossing(c, s):
        return c == 0 or s > 1

    def guard(ok, body):
        if ok is None:
            body()
        else:
            pl.when(ok)(body)

    for s in range(line - 1, -1, -1):
        for c in range(2):
            for ok, at in spots(s):
                if crossing(c, s):
                    guard(ok, lambda: ac_copy(c, parts[c].at[2 * at + 1 - col], at).start())

    @pl.when(row > 0)
    def _():
        ex_copy(0, partner, above).wait_recv()

    @pl.when(row < line - 1)
    def _():
        ex_copy(1, partner, below).wait_recv()

    @pl.when((row > 0) & (row < line - 1))
    def _():
        total(cross_buf, (b_ref.at[partner], ex_buf.at[0], ex_buf.at[1]))

    @pl.when(row == 0)
    def _():
        total(cross_buf, (b_ref.at[partner], ex_buf.at[1]))

    @pl.when((row > 0) & (row == line - 1))
    def _():
        total(cross_buf, (b_ref.at[partner], ex_buf.at[0]))

    ac_copy(1, cross_buf, row).start()

    for s in range(line - 1, 0, -1):
        for c in range(2):

            @pl.when(row + s < line)
            def _():
                at = row + s
                slot = pair_buf.at[c, at]
                mine = parts[c].at[2 * at + col]
                base = (mine,)
                if crossing(c, s):
                    ac_copy(c, mine, at).wait_recv()
                    base = (mine, slot)
                if s < line - 1:

                    @pl.when(row > 0)
                    def _():
                        up_copy(c, at).wait_recv()
                        total(slot, base + (line_buf.at[c, at],))

                @pl.when(row == 0)
                def _():
                    total(slot, base)

                up_copy(c, at).start()

            @pl.when(row >= s)
            def _():
                at = row - s
                slot = pair_buf.at[c, at]
                mine = parts[c].at[2 * at + col]
                base = (mine,)
                if crossing(c, s):
                    ac_copy(c, mine, at).wait_recv()
                    base = (mine, slot)
                if s < line - 1:

                    @pl.when(row < line - 1)
                    def _():
                        dn_copy(c, at, line_buf.at[c, at]).wait_recv()
                        total(slot, base + (line_buf.at[c, at],))

                @pl.when(row == line - 1)
                def _():
                    total(slot, base)

                if s == 1:
                    dn_copy(c, at, top_buf.at[c]).start()
                else:
                    dn_copy(c, at, line_buf.at[c, at]).start()

    for c in range(2):
        mine = parts[c].at[me]
        slot = pair_buf.at[c, row]
        from_below = line_buf.at[c, row]
        from_above = top_buf.at[c]
        ac_copy(c, mine, row).wait_recv()

        @pl.when(row > 0)
        def _():
            up_copy(c, row).wait_recv()

        @pl.when(row < line - 1)
        def _():
            dn_copy(c, row, from_above).wait_recv()

        @pl.when((row > 0) & (row < line - 1))
        def _():
            total(outs[c], (mine, slot, from_below, from_above))

        @pl.when(row == 0)
        def _():
            total(outs[c], (mine, slot, from_above))

        @pl.when((row > 0) & (row == line - 1))
        def _():
            total(outs[c], (mine, slot, from_below))

    ac_copy(0, m_ref.at[partner], row).wait_send()
    ac_copy(1, cross_buf, row).wait_send()
    for s in range(1, line):
        for c in range(2):
            for ok, at in spots(s):
                if crossing(c, s):
                    guard(ok, lambda: ac_copy(c, parts[c].at[2 * at + 1 - col], at).wait_send())

            @pl.when(row + s < line)
            def _():
                up_copy(c, row + s).wait_send()

            @pl.when(row >= s)
            def _():
                dn_copy(c, row - s, line_buf.at[c, row - s]).wait_send()

    @pl.when(row < line - 1)
    def _():
        ex_copy(0, partner + 2, above).wait_send()

    @pl.when(row > 0)
    def _():
        ex_copy(1, partner - 2, below).wait_send()


def scatter_rows(blocks, mixed_terms, back_terms):
    line = blocks // 2
    rows = mixed_terms.shape[0] // blocks
    width = mixed_terms.shape[1]
    dma = pltpu.SemaphoreType.DMA
    block = jax.ShapeDtypeStruct((rows, width), bf16)
    block_bytes = 2 * rows * width
    return pl.pallas_call(
        functools.partial(scatter_kernel, blocks),
        out_shape=(block, block),
        in_specs=[pl.BlockSpec(memory_space=pltpu.VMEM)] * 2,
        out_specs=(pl.BlockSpec(memory_space=pltpu.VMEM),) * 2,
        scratch_shapes=[
            pltpu.VMEM((2, line, rows, width), bf16),
            pltpu.VMEM((2, line, rows, width), bf16),
            pltpu.VMEM((2, rows, width), bf16),
            pltpu.VMEM((2, rows, width), bf16),
            pltpu.VMEM((rows, width), bf16),
        ]
        + [dma((2, line))] * 6
        + [dma((2,))] * 2,
        compiler_params=pltpu.CompilerParams(
            collective_id=3,
            has_side_effects=True,
            vmem_limit_bytes=block_bytes * (2 * blocks + 4 * line + 12) + 2 * 2**20,
        ),
        name="scatter_rows",
    )(
        mixed_terms.reshape(blocks, rows, width),
        back_terms.reshape(blocks, rows, width),
    )


def sum_kernel(blocks, c_ref, o_ref, land, send_sem, recv_sem):
    me = lax.axis_index("blk")
    barrier = pltpu.get_barrier_semaphore()
    for k in range(1, blocks):
        pl.semaphore_signal(
            barrier, inc=1, device_id={"blk": lax.rem(me + k, blocks)}, device_id_type=MESH
        )
    pl.semaphore_wait(barrier, blocks - 1)
    copies = []
    for k in range(1, blocks):
        copy = remote(
            c_ref, land.at[k], send_sem.at[k], recv_sem.at[k], lax.rem(me + k, blocks)
        )
        copy.start()
        copies.append(copy)
    acc = c_ref[...].astype(f32)
    for k in range(1, blocks):
        copies[k - 1].wait_recv()
        acc = acc + land[k].astype(f32)
    o_ref[...] = acc.astype(o_ref.dtype)
    for copy in copies:
        copy.wait_send()


def sum_over_blk(blocks, coeffs, collective_id):
    dma = pltpu.SemaphoreType.DMA
    return pl.pallas_call(
        functools.partial(sum_kernel, blocks),
        out_shape=jax.ShapeDtypeStruct(coeffs.shape, coeffs.dtype),
        in_specs=[pl.BlockSpec(memory_space=pltpu.VMEM)],
        out_specs=pl.BlockSpec(memory_space=pltpu.VMEM),
        scratch_shapes=[
            pltpu.VMEM((blocks,) + coeffs.shape, coeffs.dtype),
            dma((blocks,)),
            dma((blocks,)),
        ],
        compiler_params=pltpu.CompilerParams(
            collective_id=collective_id, has_side_effects=True, vmem_limit_bytes=8 * 2**20
        ),
        name="sum_over_blk",
    )(coeffs)


adapter_scale = 2.0


def silu_pair(gate_in):
    sigmoid_val = jax.nn.sigmoid(gate_in)
    return (gate_in * sigmoid_val, sigmoid_val * (1.0 + gate_in * (1.0 - sigmoid_val)))


def dot(a, b, dims=((1,), (0,))):
    return lax.dot_general(a, b, (dims, ((), ())), preferred_element_type=f32)


def ranks_pattern(rank, entries):
    column = lax.broadcasted_iota(jnp.int32, (rank, entries * rank), 1)
    row = lax.broadcasted_iota(jnp.int32, (rank, entries * rank), 0)
    return (column % rank == row).astype(bf16)


def local(
    tokens,
    cotangent,
    gate_weight,
    up_weight,
    down_weight,
    a_gate,
    a_up,
    down_output_factors,
    b_gate,
    b_up,
    a_down,
    tenant_of_row,
    adapter_slot,
):
    own_rows, width = tokens.shape
    blocks = lax.axis_size("blk")
    grp_count = lax.axis_size("grp")
    blk_index = lax.axis_index("blk")
    grp_index = lax.axis_index("grp")
    per_owner, rank = a_gate.shape[:2]
    tenant_count, _, units = b_gate.shape
    capacity = 2 * own_rows
    group_rows = own_rows * blocks
    x, dy = gather_rows(blocks, tokens, cotangent)

    layout = tenant_of_row.reshape(blocks, grp_count, own_rows)
    all_tenants = jnp.transpose(layout, (1, 0, 2)).reshape(grp_count, group_rows)
    tenant_hot = all_tenants[:, :, None] == jnp.arange(tenant_count, dtype=jnp.int32)
    all_slots = jnp.sum(jnp.where(tenant_hot, adapter_slot, 0), axis=2)
    mine = all_slots // per_owner == blk_index
    within = jnp.cumsum(mine.astype(jnp.int32), axis=1) - 1
    choose = mine[:, None, :] & (
        within[:, None, :] == jnp.arange(capacity, dtype=jnp.int32)[None, :, None]
    )
    choose_bf = choose.astype(bf16)
    picked_slot = (
        jnp.max(jnp.where(choose, all_slots[:, None, :], -1), axis=2).reshape(1, -1)
    )
    tenants = lax.dynamic_index_in_dim(all_tenants, grp_index, 0, keepdims=False)
    slots = lax.dynamic_index_in_dim(all_slots, grp_index, 0, keepdims=False)
    choose_own = lax.dynamic_index_in_dim(choose_bf, grp_index, 0, keepdims=False)

    slot_of_column = blk_index * per_owner + jnp.arange(per_owner * rank, dtype=jnp.int32) // rank
    slot_mask = slots[:, None] == slot_of_column[None, :]
    tenant_of_column = jnp.arange(tenant_count * rank, dtype=jnp.int32) // rank
    tenant_mask = tenants[:, None] == tenant_of_column[None, :]
    slot_pattern = ranks_pattern(rank, per_owner)
    tenant_pattern = ranks_pattern(rank, tenant_count)

    own_x = dot(choose_own, x).astype(bf16)
    own_dy = dot(choose_own, dy).astype(bf16)
    all_x = lax.all_gather(own_x, "grp", axis=0, tiled=True)
    all_dy = lax.all_gather(own_dy, "grp", axis=0, tiled=True)

    ag = a_gate.reshape(per_owner * rank, width)
    au = a_up.reshape(per_owner * rank, width)
    bd = down_output_factors.reshape(per_owner * rank, width)
    bg = b_gate.reshape(tenant_count * rank, units)
    bu = b_up.reshape(tenant_count * rank, units)
    ad = a_down.reshape(tenant_count * rank, units)

    def select(rows, factors, mask, pattern):
        full = dot(rows, factors, ((1,), (1,)))
        kept = jnp.where(mask, full, 0.0).astype(bf16)
        return dot(pattern, kept, ((1,), (1,)))

    def spread(coeffs, mask, pattern):
        return jnp.where(mask, dot(coeffs, pattern, ((0,), (0,))), 0.0).astype(bf16)

    low_in = jnp.concatenate(
        (
            select(x, ag, slot_mask, slot_pattern),
            select(x, au, slot_mask, slot_pattern),
            adapter_scale * select(dy, bd, slot_mask, slot_pattern),
        ),
        axis=0,
    ).astype(bf16)
    coeffs = sum_over_blk(blocks, low_in, 1)
    p_gate, p_up, grad_q = coeffs[:rank], coeffs[rank : 2 * rank], coeffs[2 * rank :]

    twice = jnp.asarray(adapter_scale, bf16)
    gate_val = dot(x, gate_weight) + dot(spread(twice * p_gate, tenant_mask, tenant_pattern), bg)
    up_val = dot(x, up_weight) + dot(spread(twice * p_up, tenant_mask, tenant_pattern), bu)
    grad_h = dot(dy, down_weight, ((1,), (1,))) + dot(
        spread(grad_q, tenant_mask, tenant_pattern), ad
    )
    act_val, act_slope = silu_pair(gate_val)
    hidden = (act_val * up_val).astype(bf16)
    grad_gate = (grad_h * up_val * act_slope).astype(bf16)
    grad_up = (grad_h * act_val).astype(bf16)

    low_out = jnp.concatenate(
        (
            select(hidden, ad, tenant_mask, tenant_pattern),
            adapter_scale * select(grad_gate, bg, tenant_mask, tenant_pattern),
            adapter_scale * select(grad_up, bu, tenant_mask, tenant_pattern),
        ),
        axis=0,
    ).astype(bf16)
    sums = sum_over_blk(blocks, low_out, 2)
    low_q, dp_gate, dp_up = sums[:rank], sums[rank : 2 * rank], sums[2 * rank :]

    small = jnp.transpose(jnp.concatenate((coeffs, sums), axis=0))
    packed = jnp.concatenate((hidden, grad_gate, grad_up, small), axis=1)
    spare = -packed.shape[1] % 128
    packed = jnp.pad(packed, ((0, 0), (0, spare)))
    everyone = lax.all_gather(packed, "grp", axis=0, tiled=True)

    out_rows = dot(hidden, down_weight) + dot(
        spread(twice * low_q, slot_mask, slot_pattern), bd
    )
    back_in = (
        dot(grad_gate, gate_weight, ((1,), (1,)))
        + dot(grad_up, up_weight, ((1,), (1,)))
        + dot(spread(dp_gate, slot_mask, slot_pattern), ag)
        + dot(spread(dp_up, slot_mask, slot_pattern), au)
    )
    mixed, input_grad = scatter_rows(blocks, out_rows.astype(bf16), back_in.astype(bf16))

    all_small = everyone[:, 3 * units : 3 * units + 6 * rank]
    picked = jnp.einsum(
        "gcn,gnk->gck",
        choose_bf,
        all_small[:, 3 * rank :].reshape(grp_count, group_rows, 3 * rank),
        preferred_element_type=f32,
    ).astype(bf16)
    picked = picked.reshape(grp_count * capacity, 3 * rank)
    slots_dev = per_owner // grp_count
    first_slot = blk_index * per_owner + grp_index * slots_dev
    slot_of_line = first_slot + jnp.arange(slots_dev * rank, dtype=jnp.int32) // rank
    line_mask = slot_of_line[:, None] == picked_slot
    line_pattern = ranks_pattern(rank, slots_dev)

    def slot_grad(values, entries):
        weights = dot(line_pattern, values, ((0,), (1,)))
        weights = jnp.where(line_mask, weights, 0.0).astype(bf16)
        return dot(weights, entries).reshape(slots_dev, rank, width)

    grad_bd = slot_grad(twice * picked[:, :rank], all_dy)
    grad_ag = slot_grad(picked[:, rank : 2 * rank], all_x)
    grad_au = slot_grad(picked[:, 2 * rank :], all_x)

    tenant_dev = tenant_count // grp_count
    tenant_of_line = grp_index * tenant_dev + jnp.arange(tenant_dev * rank, dtype=jnp.int32) // rank
    member = tenant_of_line[:, None] == all_tenants.reshape(1, -1)
    member_pattern = ranks_pattern(rank, tenant_dev)

    def tenant_grad(values, entries):
        weights = dot(member_pattern, values, ((0,), (1,)))
        weights = jnp.where(member, weights, 0.0).astype(bf16)
        return dot(weights, entries).reshape(tenant_dev, rank, units)

    grad_bg = tenant_grad(twice * all_small[:, :rank], everyone[:, units : 2 * units])
    grad_bu = tenant_grad(
        twice * all_small[:, rank : 2 * rank], everyone[:, 2 * units : 3 * units]
    )
    grad_ad = tenant_grad(all_small[:, 2 * rank : 3 * rank], everyone[:, :units])
    return (mixed, input_grad, grad_ag, grad_au, grad_bd, grad_bg, grad_bu, grad_ad)


def solution(mesh):
    placed = (
        P(("blk", "grp"), None),
        P(("blk", "grp"), None),
        P(None, "blk"),
        P(None, "blk"),
        P("blk", None),
        P("blk", None, None),
        P("blk", None, None),
        P("blk", None, None),
        P(None, None, "blk"),
        P(None, None, "blk"),
        P(None, None, "blk"),
        P(),
        P(),
    )
    return jax.shard_map(
        local,
        mesh=mesh,
        in_specs=placed,
        out_specs=(
            P(("blk", "grp"), None),
            P(("blk", "grp"), None),
            P(("blk", "grp"), None, None),
            P(("blk", "grp"), None, None),
            P(("blk", "grp"), None, None),
            P("grp", None, "blk"),
            P("grp", None, "blk"),
            P("grp", None, "blk"),
        ),
        check_vma=False,
    )
```

```python
import functools

import jax
import jax.numpy as jnp
from jax import lax
from jax.experimental import pallas as pl
from jax.experimental.pallas import tpu as pltpu
from jax.sharding import PartitionSpec as P

MESH = pl.DeviceIdType.MESH
bf16 = jnp.bfloat16
f32 = jnp.float32


def remote(src, dst, send, recv, to):
    return pltpu.make_async_remote_copy(
        src_ref=src,
        dst_ref=dst,
        send_sem=send,
        recv_sem=recv,
        device_id={"blk": to},
        device_id_type=MESH,
    )


def place(blocks):
    me = lax.axis_index("blk")
    line = blocks // 2
    row = me // 2
    col = me - 2 * row
    partner = me + 1 - 2 * col
    return me, line, row, col, partner


def greet(me, line, row, partner):
    barrier = pltpu.get_barrier_semaphore()
    pl.semaphore_signal(barrier, inc=1, device_id={"blk": partner}, device_id_type=MESH)

    @pl.when(row < line - 1)
    def _():
        pl.semaphore_signal(barrier, inc=1, device_id={"blk": me + 2}, device_id_type=MESH)

    @pl.when(row > 0)
    def _():
        pl.semaphore_signal(barrier, inc=1, device_id={"blk": me - 2}, device_id_type=MESH)

    peers = 1 + (row < line - 1).astype(jnp.int32) + (row > 0).astype(jnp.int32)
    pl.semaphore_wait(barrier, peers)


def gather_kernel(
    blocks, x_ref, d_ref, xo_ref, do_ref, own_sem, up_s, up_r, dn_s, dn_r, ac_s, ac_r, ex_s, ex_r
):
    me, line, row, col, partner = place(blocks)
    outs = (xo_ref, do_ref)
    ins = (x_ref, d_ref)
    above, below = me + 2, me - 2

    def up_copy(c, src, block, s):
        return remote(src, outs[c].at[block], up_s.at[c, s], up_r.at[c, s], above)

    def dn_copy(c, src, block, s):
        return remote(src, outs[c].at[block], dn_s.at[c, s], dn_r.at[c, s], below)

    def ac_copy(c, src, at):
        return remote(
            src, outs[c].at[2 * at + col], ac_s.at[c, at], ac_r.at[c, at], partner
        )

    def ac_arrival(c, at):
        ref = outs[c].at[2 * at + 1 - col]
        return remote(ref, ref, ac_s.at[c, at], ac_r.at[c, at], partner)

    def ex_copy(direction, to):
        ref = do_ref.at[partner]
        return remote(ref, ref, ex_s.at[direction], ex_r.at[direction], to)

    def ex_arrival(direction, block, to):
        ref = do_ref.at[block]
        return remote(ref, ref, ex_s.at[direction], ex_r.at[direction], to)

    greet(me, line, row, partner)
    own = []
    for c in range(2):
        ac_copy(c, ins[c], row).start()

        @pl.when(row < line - 1)
        def _():
            up_copy(c, ins[c], me, 0).start()

        @pl.when(row > 0)
        def _():
            dn_copy(c, ins[c], me, 0).start()

    for c in range(2):
        copy = pltpu.make_async_copy(ins[c], outs[c].at[me], own_sem.at[c])
        copy.start()
        own.append(copy)
    for s in range(1, line):
        for c in range(2):

            @pl.when(row >= s)
            def _():
                block = me - 2 * s
                ref = outs[c].at[block]
                up_copy(c, ref, block, s - 1).wait_recv()
                if s < line - 1:

                    @pl.when(row < line - 1)
                    def _():
                        up_copy(c, ref, block, s).start()

                if c == 0 or s > 1:
                    ac_copy(c, ref, row - s).start()

            @pl.when(row + s < line)
            def _():
                block = me + 2 * s
                ref = outs[c].at[block]
                dn_copy(c, ref, block, s - 1).wait_recv()
                if s < line - 1:

                    @pl.when(row > 0)
                    def _():
                        dn_copy(c, ref, block, s).start()

                if c == 0 or s > 1:
                    ac_copy(c, ref, row + s).start()

        if s == 1:
            ac_arrival(1, row).wait_recv()

            @pl.when(row < line - 1)
            def _():
                ex_copy(0, above).start()

            @pl.when(row > 0)
            def _():
                ex_copy(1, below).start()

    ac_arrival(0, row).wait_recv()
    ac_copy(0, x_ref, row).wait_send()
    ac_copy(1, d_ref, row).wait_send()
    for s in range(1, line):
        for c in range(2):
            for ok, at in ((row >= s, row - s), (row + s < line, row + s)):

                @pl.when(ok)
                def _():
                    if c == 0 or s > 1:
                        ac_arrival(c, at).wait_recv()
                        ac_copy(c, outs[c].at[2 * at + col], at).wait_send()

    @pl.when(row > 0)
    def _():
        ex_arrival(0, partner - 2, above).wait_recv()
        ex_copy(1, below).wait_send()

    @pl.when(row < line - 1)
    def _():
        ex_arrival(1, partner + 2, below).wait_recv()
        ex_copy(0, above).wait_send()

    for s in range(line - 1):
        for c in range(2):

            @pl.when((row >= s) & (row < line - 1))
            def _():
                src = ins[c] if s == 0 else outs[c].at[me - 2 * s]
                up_copy(c, src, me - 2 * s, s).wait_send()

            @pl.when((row + s < line) & (row > 0))
            def _():
                src = ins[c] if s == 0 else outs[c].at[me + 2 * s]
                dn_copy(c, src, me + 2 * s, s).wait_send()

    for copy in own:
        copy.wait()


def gather_rows(blocks, x, dy):
    line = blocks // 2
    shape = jax.ShapeDtypeStruct((blocks,) + x.shape, x.dtype)
    dma = pltpu.SemaphoreType.DMA
    got = pl.pallas_call(
        functools.partial(gather_kernel, blocks),
        out_shape=(shape, shape),
        in_specs=[pl.BlockSpec(memory_space=pl.ANY)] * 2,
        out_specs=(pl.BlockSpec(memory_space=pl.ANY),) * 2,
        scratch_shapes=[dma((2,))] + [dma((2, line))] * 6 + [dma((2,))] * 2,
        compiler_params=pltpu.CompilerParams(
            collective_id=0, has_side_effects=True, vmem_limit_bytes=4 * 2**20
        ),
        name="gather_rows",
    )(x, dy)
    return [part.reshape((-1,) + x.shape[1:]) for part in got]


def scatter_kernel(
    blocks,
    m_ref,
    b_ref,
    mo_ref,
    bo_ref,
    pair_buf,
    line_buf,
    top_buf,
    ex_buf,
    cross_buf,
    ac_s,
    ac_r,
    up_s,
    up_r,
    dn_s,
    dn_r,
    ex_s,
    ex_r,
):
    me, line, row, col, partner = place(blocks)
    parts = (m_ref, b_ref)
    outs = (mo_ref, bo_ref)
    above, below = me + 2, me - 2
    width = m_ref.shape[-1]
    tile = width // 8

    def total(dst, srcs):
        def body(k, carry):
            at = pl.ds(pl.multiple_of(k * tile, tile), tile)
            acc = srcs[0][:, at].astype(f32)
            for src in srcs[1:]:
                acc = acc + src[:, at].astype(f32)
            dst[:, at] = acc.astype(dst.dtype)
            return carry

        lax.fori_loop(0, width // tile, body, 0)

    def ac_copy(c, src, at):
        return remote(src, pair_buf.at[c, at], ac_s.at[c, at], ac_r.at[c, at], partner)

    def up_copy(c, at):
        return remote(
            pair_buf.at[c, at], line_buf.at[c, at], up_s.at[c, at], up_r.at[c, at], above
        )

    def dn_copy(c, at, landing):
        return remote(pair_buf.at[c, at], landing, dn_s.at[c, at], dn_r.at[c, at], below)

    def ex_copy(direction, block, to):
        return remote(
            b_ref.at[block], ex_buf.at[direction], ex_s.at[direction], ex_r.at[direction], to
        )

    greet(me, line, row, partner)

    @pl.when(row < line - 1)
    def _():
        ex_copy(0, partner + 2, above).start()

    @pl.when(row > 0)
    def _():
        ex_copy(1, partner - 2, below).start()

    def spots(s):
        if s == 0:
            return ((None, row),)
        return ((row + s < line, row + s), (row >= s, row - s))

    def crossing(c, s):
        return c == 0 or s > 1

    def guard(ok, body):
        if ok is None:
            body()
        else:
            pl.when(ok)(body)

    for s in range(line - 1, -1, -1):
        for c in range(2):
            for ok, at in spots(s):
                if crossing(c, s):
                    guard(ok, lambda: ac_copy(c, parts[c].at[2 * at + 1 - col], at).start())

    @pl.when(row > 0)
    def _():
        ex_copy(0, partner, above).wait_recv()

    @pl.when(row < line - 1)
    def _():
        ex_copy(1, partner, below).wait_recv()

    @pl.when((row > 0) & (row < line - 1))
    def _():
        total(cross_buf, (b_ref.at[partner], ex_buf.at[0], ex_buf.at[1]))

    @pl.when(row == 0)
    def _():
        total(cross_buf, (b_ref.at[partner], ex_buf.at[1]))

    @pl.when((row > 0) & (row == line - 1))
    def _():
        total(cross_buf, (b_ref.at[partner], ex_buf.at[0]))

    ac_copy(1, cross_buf, row).start()

    for s in range(line - 1, 0, -1):
        for c in range(2):

            @pl.when(row + s < line)
            def _():
                at = row + s
                slot = pair_buf.at[c, at]
                mine = parts[c].at[2 * at + col]
                base = (mine,)
                if crossing(c, s):
                    ac_copy(c, mine, at).wait_recv()
                    base = (mine, slot)
                if s < line - 1:

                    @pl.when(row > 0)
                    def _():
                        up_copy(c, at).wait_recv()
                        total(slot, base + (line_buf.at[c, at],))

                @pl.when(row == 0)
                def _():
                    total(slot, base)

                up_copy(c, at).start()

            @pl.when(row >= s)
            def _():
                at = row - s
                slot = pair_buf.at[c, at]
                mine = parts[c].at[2 * at + col]
                base = (mine,)
                if crossing(c, s):
                    ac_copy(c, mine, at).wait_recv()
                    base = (mine, slot)
                if s < line - 1:

                    @pl.when(row < line - 1)
                    def _():
                        dn_copy(c, at, line_buf.at[c, at]).wait_recv()
                        total(slot, base + (line_buf.at[c, at],))

                @pl.when(row == line - 1)
                def _():
                    total(slot, base)

                if s == 1:
                    dn_copy(c, at, top_buf.at[c]).start()
                else:
                    dn_copy(c, at, line_buf.at[c, at]).start()

    for c in range(2):
        mine = parts[c].at[me]
        slot = pair_buf.at[c, row]
        from_below = line_buf.at[c, row]
        from_above = top_buf.at[c]
        ac_copy(c, mine, row).wait_recv()

        @pl.when(row > 0)
        def _():
            up_copy(c, row).wait_recv()

        @pl.when(row < line - 1)
        def _():
            dn_copy(c, row, from_above).wait_recv()

        @pl.when((row > 0) & (row < line - 1))
        def _():
            total(outs[c], (mine, slot, from_below, from_above))

        @pl.when(row == 0)
        def _():
            total(outs[c], (mine, slot, from_above))

        @pl.when((row > 0) & (row == line - 1))
        def _():
            total(outs[c], (mine, slot, from_below))

    ac_copy(0, m_ref.at[partner], row).wait_send()
    ac_copy(1, cross_buf, row).wait_send()
    for s in range(1, line):
        for c in range(2):
            for ok, at in spots(s):
                if crossing(c, s):
                    guard(ok, lambda: ac_copy(c, parts[c].at[2 * at + 1 - col], at).wait_send())

            @pl.when(row + s < line)
            def _():
                up_copy(c, row + s).wait_send()

            @pl.when(row >= s)
            def _():
                dn_copy(c, row - s, line_buf.at[c, row - s]).wait_send()

    @pl.when(row < line - 1)
    def _():
        ex_copy(0, partner + 2, above).wait_send()

    @pl.when(row > 0)
    def _():
        ex_copy(1, partner - 2, below).wait_send()


def scatter_rows(blocks, mixed_terms, back_terms):
    line = blocks // 2
    rows = mixed_terms.shape[0] // blocks
    width = mixed_terms.shape[1]
    dma = pltpu.SemaphoreType.DMA
    block = jax.ShapeDtypeStruct((rows, width), bf16)
    block_bytes = 2 * rows * width
    return pl.pallas_call(
        functools.partial(scatter_kernel, blocks),
        out_shape=(block, block),
        in_specs=[pl.BlockSpec(memory_space=pltpu.VMEM)] * 2,
        out_specs=(pl.BlockSpec(memory_space=pltpu.VMEM),) * 2,
        scratch_shapes=[
            pltpu.VMEM((2, line, rows, width), bf16),
            pltpu.VMEM((2, line, rows, width), bf16),
            pltpu.VMEM((2, rows, width), bf16),
            pltpu.VMEM((2, rows, width), bf16),
            pltpu.VMEM((rows, width), bf16),
        ]
        + [dma((2, line))] * 6
        + [dma((2,))] * 2,
        compiler_params=pltpu.CompilerParams(
            collective_id=3,
            has_side_effects=True,
            vmem_limit_bytes=block_bytes * (2 * blocks + 4 * line + 12) + 2 * 2**20,
        ),
        name="scatter_rows",
    )(
        mixed_terms.reshape(blocks, rows, width),
        back_terms.reshape(blocks, rows, width),
    )


def sum_kernel(blocks, c_ref, o_ref, land, send_sem, recv_sem):
    me = lax.axis_index("blk")
    barrier = pltpu.get_barrier_semaphore()
    for k in range(1, blocks):
        pl.semaphore_signal(
            barrier, inc=1, device_id={"blk": lax.rem(me + k, blocks)}, device_id_type=MESH
        )
    pl.semaphore_wait(barrier, blocks - 1)
    copies = []
    for k in range(1, blocks):
        copy = remote(
            c_ref, land.at[k], send_sem.at[k], recv_sem.at[k], lax.rem(me + k, blocks)
        )
        copy.start()
        copies.append(copy)
    acc = c_ref[...].astype(f32)
    for k in range(1, blocks):
        copies[k - 1].wait_recv()
        acc = acc + land[k].astype(f32)
    o_ref[...] = acc.astype(o_ref.dtype)
    for copy in copies:
        copy.wait_send()


def sum_over_blk(blocks, coeffs, collective_id):
    dma = pltpu.SemaphoreType.DMA
    return pl.pallas_call(
        functools.partial(sum_kernel, blocks),
        out_shape=jax.ShapeDtypeStruct(coeffs.shape, coeffs.dtype),
        in_specs=[pl.BlockSpec(memory_space=pltpu.VMEM)],
        out_specs=pl.BlockSpec(memory_space=pltpu.VMEM),
        scratch_shapes=[
            pltpu.VMEM((blocks,) + coeffs.shape, coeffs.dtype),
            dma((blocks,)),
            dma((blocks,)),
        ],
        compiler_params=pltpu.CompilerParams(
            collective_id=collective_id, has_side_effects=True, vmem_limit_bytes=8 * 2**20
        ),
        name="sum_over_blk",
    )(coeffs)


adapter_scale = 2.0


def silu_pair(gate_in):
    sigmoid_val = jax.nn.sigmoid(gate_in)
    return (gate_in * sigmoid_val, sigmoid_val * (1.0 + gate_in * (1.0 - sigmoid_val)))


def dot(a, b, dims=((1,), (0,))):
    return lax.dot_general(a, b, (dims, ((), ())), preferred_element_type=f32)


def ranks_pattern(rank, entries):
    column = lax.broadcasted_iota(jnp.int32, (rank, entries * rank), 1)
    row = lax.broadcasted_iota(jnp.int32, (rank, entries * rank), 0)
    return (column % rank == row).astype(bf16)


def lanes_entry(rank, first, count):
    return (lax.broadcasted_iota(jnp.int32, (1, count), 1) // rank) + first


def spread_kernel(coeffs, mask, pattern):
    return jnp.where(mask, dot(coeffs, pattern), 0.0).astype(bf16)


def select_kernel(full, mask, pattern):
    kept = jnp.where(mask, full, 0.0).astype(bf16)
    return dot(pattern, kept, ((1,), (1,)))


def inputs_kernel(
    rank, x, d, gw, uw, dw, ag, au, bd, slot, pat, gate_o, up_o, gh_o, low_o, qg, qu, qd
):
    step = pl.program_id(0)
    xv, dv = x[...], d[...]
    terms = (
        (gate_o, lambda: dot(xv, gw[...])),
        (up_o, lambda: dot(xv, uw[...])),
        (gh_o, lambda: dot(dv, dw[...], ((1,), (1,)))),
        (qg, lambda: dot(xv, ag[...], ((1,), (1,)))),
        (qu, lambda: dot(xv, au[...], ((1,), (1,)))),
        (qd, lambda: dot(dv, bd[...], ((1,), (1,)))),
    )

    @pl.when(step == 0)
    def _():
        for ref, _term in terms:
            ref[...] = jnp.zeros_like(ref)

    for ref, term in terms:
        ref[...] += term()

    @pl.when(step == pl.num_programs(0) - 1)
    def _():
        mask = slot[...] == lanes_entry(rank, 0, qg.shape[1])
        for k, (ref, scale) in enumerate(((qg, 1.0), (qu, 1.0), (qd, adapter_scale))):
            low_o[k * rank : (k + 1) * rank, :] = (
                scale * select_kernel(ref[...], mask, pat[...])
            ).astype(bf16)


def input_terms(rank, x, dy, gw, uw, dw, ag, au, bd, slot, pat):
    rows, width = x.shape
    units, own = gw.shape[1], ag.shape[0]
    tile = min(512, width)
    across = lambda n: pl.BlockSpec((n, tile), lambda i: (0, i))
    down = lambda n: pl.BlockSpec((tile, n), lambda i: (i, 0))
    whole = lambda *shape: pl.BlockSpec(shape, lambda i: (0, 0))
    acc = jax.ShapeDtypeStruct((rows, units), f32)
    return pl.pallas_call(
        functools.partial(inputs_kernel, rank),
        grid=(width // tile,),
        out_shape=(acc, acc, acc, jax.ShapeDtypeStruct((3 * rank, rows), bf16)),
        in_specs=[
            across(rows),
            across(rows),
            down(units),
            down(units),
            across(units),
            across(own),
            across(own),
            across(own),
            whole(rows, 1),
            whole(*pat.shape),
        ],
        out_specs=(whole(rows, units),) * 3 + (whole(3 * rank, rows),),
        scratch_shapes=[pltpu.VMEM((rows, own), f32)] * 3,
        compiler_params=pltpu.CompilerParams(vmem_limit_bytes=32 * 2**20),
        cost_estimate=pl.CostEstimate(
            flops=6 * rows * width * (units + own),
            bytes_accessed=6 * width * (units + own),
            transcendentals=0,
        ),
        name="input_terms",
    )(x, dy, gw, uw, dw, ag, au, bd, slot, pat)


def middle_kernel(
    rank, gate, up, gh, coeffs, tenant, pat, bg, bu, ad, hid_o, gg_o, gu_o, low_o, sg, su, sh, low
):
    half, step = pl.program_id(0), pl.program_id(1)
    last = pl.num_programs(1) - 1
    count = bg.shape[0]
    mask = tenant[...] == lanes_entry(rank, step * (count // rank), count)

    @pl.when((half == 0) & (step == 0))
    def _():
        sg[...] = gate[...]
        su[...] = up[...]
        sh[...] = gh[...]

    @pl.when(half == 0)
    def _():
        for k, (acc, fac, scale) in enumerate(
            ((sg, bg, adapter_scale), (su, bu, adapter_scale), (sh, ad, 1.0))
        ):
            given = coeffs[:, k * rank : (k + 1) * rank]
            acc[...] += scale * dot(spread_kernel(given, mask, pat[...]), fac[...])

    @pl.when((half == 0) & (step == last))
    def _():
        act_val, act_slope = silu_pair(sg[...])
        up_val, grad_h = su[...], sh[...]
        hid_o[...] = (act_val * up_val).astype(bf16)
        gg_o[...] = (grad_h * up_val * act_slope).astype(bf16)
        gu_o[...] = (grad_h * act_val).astype(bf16)
        low[...] = jnp.zeros_like(low)

    @pl.when(half == 1)
    def _():
        for k, (rows, fac, scale) in enumerate(
            ((hid_o, ad, 1.0), (gg_o, bg, adapter_scale), (gu_o, bu, adapter_scale))
        ):
            full = dot(rows[...], fac[...], ((1,), (1,)))
            low[k * rank : (k + 1) * rank, :] += scale * select_kernel(full, mask, pat[...])

    @pl.when((half == 1) & (step == last))
    def _():
        low_o[...] = low[...].astype(bf16)


def middle_terms(rank, gate, up, gh, coeffs, tenant, bg, bu, ad):
    rows, units = gate.shape
    total = bg.shape[0]
    tile = min(1024, total)
    pat = ranks_pattern(rank, tile // rank)
    whole = lambda *shape: pl.BlockSpec(shape, lambda h, i: (0, 0))
    down = pl.BlockSpec((tile, units), lambda h, i: (i, 0))
    block = jax.ShapeDtypeStruct((rows, units), bf16)
    return pl.pallas_call(
        functools.partial(middle_kernel, rank),
        grid=(2, total // tile),
        out_shape=(block, block, block, jax.ShapeDtypeStruct((3 * rank, rows), bf16)),
        in_specs=[whole(rows, units)] * 3
        + [whole(rows, 3 * rank), whole(rows, 1), whole(*pat.shape)]
        + [down] * 3,
        out_specs=(whole(rows, units),) * 3 + (whole(3 * rank, rows),),
        scratch_shapes=[pltpu.VMEM((rows, units), f32)] * 3
        + [pltpu.VMEM((3 * rank, rows), f32)],
        compiler_params=pltpu.CompilerParams(vmem_limit_bytes=32 * 2**20),
        cost_estimate=pl.CostEstimate(
            flops=12 * rows * total * units,
            bytes_accessed=12 * total * units,
            transcendentals=rows * units,
        ),
        name="middle_terms",
    )(gate, up, gh, coeffs, tenant, pat, bg, bu, ad)


def outputs_kernel(
    rank, hid, gg, gu, sums, slot, pat, gw, uw, dw, ag, au, bd, mixed_o, back_o, eq, eg, eu
):
    @pl.when(pl.program_id(0) == 0)
    def _():
        mask = slot[...] == lanes_entry(rank, 0, eq.shape[1])
        for k, (ref, scale) in enumerate(((eq, adapter_scale), (eg, 1.0), (eu, 1.0))):
            given = sums[:, k * rank : (k + 1) * rank]
            ref[...] = (
                scale * jnp.where(mask, dot(given, pat[...]), 0.0)
            ).astype(bf16)

    mixed_o[...] = (dot(hid[...], dw[...]) + dot(eq[...], bd[...])).astype(bf16)
    back_o[...] = (
        dot(gg[...], gw[...], ((1,), (1,)))
        + dot(gu[...], uw[...], ((1,), (1,)))
        + dot(eg[...], ag[...])
        + dot(eu[...], au[...])
    ).astype(bf16)


def output_terms(rank, hid, gg, gu, sums, slot, pat, gw, uw, dw, ag, au, bd):
    rows, units = hid.shape
    width, own = ag.shape[1], ag.shape[0]
    tile = min(512, width)
    across = lambda n: pl.BlockSpec((n, tile), lambda i: (0, i))
    down = lambda n: pl.BlockSpec((tile, n), lambda i: (i, 0))
    whole = lambda *shape: pl.BlockSpec(shape, lambda i: (0, 0))
    block = jax.ShapeDtypeStruct((rows, width), bf16)
    return pl.pallas_call(
        functools.partial(outputs_kernel, rank),
        grid=(width // tile,),
        out_shape=(block, block),
        in_specs=[whole(rows, units)] * 3
        + [whole(rows, 3 * rank), whole(rows, 1), whole(*pat.shape)]
        + [down(units), down(units), across(units), across(own), across(own), across(own)],
        out_specs=(across(rows), across(rows)),
        scratch_shapes=[pltpu.VMEM((rows, own), bf16)] * 3,
        compiler_params=pltpu.CompilerParams(vmem_limit_bytes=32 * 2**20),
        cost_estimate=pl.CostEstimate(
            flops=6 * rows * width * (units + own),
            bytes_accessed=6 * width * (units + own),
            transcendentals=0,
        ),
        name="output_terms",
    )(hid, gg, gu, sums, slot, pat, gw, uw, dw, ag, au, bd)


def local(
    tokens,
    cotangent,
    gate_weight,
    up_weight,
    down_weight,
    a_gate,
    a_up,
    down_output_factors,
    b_gate,
    b_up,
    a_down,
    tenant_of_row,
    adapter_slot,
):
    own_rows, width = tokens.shape
    blocks = lax.axis_size("blk")
    grp_count = lax.axis_size("grp")
    blk_index = lax.axis_index("blk")
    grp_index = lax.axis_index("grp")
    per_owner, rank = a_gate.shape[:2]
    tenant_count, _, units = b_gate.shape
    capacity = 2 * own_rows
    group_rows = own_rows * blocks
    x, dy = gather_rows(blocks, tokens, cotangent)

    layout = tenant_of_row.reshape(blocks, grp_count, own_rows)
    all_tenants = jnp.transpose(layout, (1, 0, 2)).reshape(grp_count, group_rows)
    tenant_hot = all_tenants[:, :, None] == jnp.arange(tenant_count, dtype=jnp.int32)
    all_slots = jnp.sum(jnp.where(tenant_hot, adapter_slot, 0), axis=2)
    mine = all_slots // per_owner == blk_index
    within = jnp.cumsum(mine.astype(jnp.int32), axis=1) - 1
    choose = mine[:, None, :] & (
        within[:, None, :] == jnp.arange(capacity, dtype=jnp.int32)[None, :, None]
    )
    choose_bf = choose.astype(bf16)
    picked_slot = (
        jnp.max(jnp.where(choose, all_slots[:, None, :], -1), axis=2).reshape(1, -1)
    )
    tenants = lax.dynamic_index_in_dim(all_tenants, grp_index, 0, keepdims=False)
    slots = lax.dynamic_index_in_dim(all_slots, grp_index, 0, keepdims=False)
    choose_own = lax.dynamic_index_in_dim(choose_bf, grp_index, 0, keepdims=False)

    local_slot = (slots - blk_index * per_owner)[:, None]
    slot_pattern = ranks_pattern(rank, per_owner)

    own_x = dot(choose_own, x).astype(bf16)
    own_dy = dot(choose_own, dy).astype(bf16)

    ag = a_gate.reshape(per_owner * rank, width)
    au = a_up.reshape(per_owner * rank, width)
    bd = down_output_factors.reshape(per_owner * rank, width)
    bg = b_gate.reshape(tenant_count * rank, units)
    bu = b_up.reshape(tenant_count * rank, units)
    ad = a_down.reshape(tenant_count * rank, units)

    gate_in, up_in, grad_in, low_in = input_terms(
        rank, x, dy, gate_weight, up_weight, down_weight, ag, au, bd, local_slot, slot_pattern
    )
    low_in, own_x, own_dy = lax.optimization_barrier((low_in, own_x, own_dy))
    all_x = lax.all_gather(own_x, "grp", axis=0, tiled=True)
    all_dy = lax.all_gather(own_dy, "grp", axis=0, tiled=True)
    twice = jnp.asarray(adapter_scale, bf16)
    coeffs = jnp.transpose(sum_over_blk(blocks, low_in, 1))
    hidden, grad_gate, grad_up, low_out = middle_terms(
        rank, gate_in, up_in, grad_in, coeffs, tenants[:, None], bg, bu, ad
    )
    sums = jnp.transpose(sum_over_blk(blocks, low_out, 2))

    packed = jnp.concatenate((hidden, grad_gate, grad_up, coeffs, sums), axis=1)
    spare = -packed.shape[1] % 128
    packed = jnp.pad(packed, ((0, 0), (0, spare)))
    everyone = lax.all_gather(packed, "grp", axis=0, tiled=True)

    mixed_terms, back_terms = output_terms(
        rank,
        hidden,
        grad_gate,
        grad_up,
        sums,
        local_slot,
        slot_pattern,
        gate_weight,
        up_weight,
        down_weight,
        ag,
        au,
        bd,
    )
    mixed, input_grad = scatter_rows(blocks, mixed_terms, back_terms)

    all_small = everyone[:, 3 * units : 3 * units + 6 * rank]
    picked = jnp.einsum(
        "gcn,gnk->gck",
        choose_bf,
        all_small[:, 3 * rank :].reshape(grp_count, group_rows, 3 * rank),
        preferred_element_type=f32,
    ).astype(bf16)
    picked = picked.reshape(grp_count * capacity, 3 * rank)
    slots_dev = per_owner // grp_count
    first_slot = blk_index * per_owner + grp_index * slots_dev
    slot_of_line = first_slot + jnp.arange(slots_dev * rank, dtype=jnp.int32) // rank
    line_mask = slot_of_line[:, None] == picked_slot
    line_pattern = ranks_pattern(rank, slots_dev)

    def slot_grad(values, entries):
        weights = dot(line_pattern, values, ((0,), (1,)))
        weights = jnp.where(line_mask, weights, 0.0).astype(bf16)
        return dot(weights, entries).reshape(slots_dev, rank, width)

    grad_bd = slot_grad(twice * picked[:, :rank], all_dy)
    grad_ag = slot_grad(picked[:, rank : 2 * rank], all_x)
    grad_au = slot_grad(picked[:, 2 * rank :], all_x)

    tenant_dev = tenant_count // grp_count
    tenant_of_line = grp_index * tenant_dev + jnp.arange(tenant_dev * rank, dtype=jnp.int32) // rank
    member = tenant_of_line[:, None] == all_tenants.reshape(1, -1)
    member_pattern = ranks_pattern(rank, tenant_dev)

    def tenant_grad(values, entries):
        weights = dot(member_pattern, values, ((0,), (1,)))
        weights = jnp.where(member, weights, 0.0).astype(bf16)
        return dot(weights, entries).reshape(tenant_dev, rank, units)

    grad_bg = tenant_grad(twice * all_small[:, :rank], everyone[:, units : 2 * units])
    grad_bu = tenant_grad(
        twice * all_small[:, rank : 2 * rank], everyone[:, 2 * units : 3 * units]
    )
    grad_ad = tenant_grad(all_small[:, 2 * rank : 3 * rank], everyone[:, :units])
    return (mixed, input_grad, grad_ag, grad_au, grad_bd, grad_bg, grad_bu, grad_ad)


def solution(mesh):
    placed = (
        P(("blk", "grp"), None),
        P(("blk", "grp"), None),
        P(None, "blk"),
        P(None, "blk"),
        P("blk", None),
        P("blk", None, None),
        P("blk", None, None),
        P("blk", None, None),
        P(None, None, "blk"),
        P(None, None, "blk"),
        P(None, None, "blk"),
        P(),
        P(),
    )
    return jax.shard_map(
        local,
        mesh=mesh,
        in_specs=placed,
        out_specs=(
            P(("blk", "grp"), None),
            P(("blk", "grp"), None),
            P(("blk", "grp"), None, None),
            P(("blk", "grp"), None, None),
            P(("blk", "grp"), None, None),
            P("grp", None, "blk"),
            P("grp", None, "blk"),
            P("grp", None, "blk"),
        ),
        check_vma=False,
    )
```

```python
import functools

import jax
import jax.numpy as jnp
from jax import lax
from jax.experimental import pallas as pl
from jax.experimental.pallas import tpu as pltpu
from jax.sharding import PartitionSpec as P

MESH = pl.DeviceIdType.MESH
bf16 = jnp.bfloat16
vmem_grant = 60 * 2**20
f32 = jnp.float32


def remote(src, dst, send, recv, to):
    return pltpu.make_async_remote_copy(
        src_ref=src,
        dst_ref=dst,
        send_sem=send,
        recv_sem=recv,
        device_id={"blk": to},
        device_id_type=MESH,
    )


def place(blocks):
    me = lax.axis_index("blk")
    line = blocks // 2
    row = me // 2
    col = me - 2 * row
    partner = me + 1 - 2 * col
    return me, line, row, col, partner


def greet(me, line, row, partner):
    barrier = pltpu.get_barrier_semaphore()
    pl.semaphore_signal(barrier, inc=1, device_id={"blk": partner}, device_id_type=MESH)

    @pl.when(row < line - 1)
    def _():
        pl.semaphore_signal(barrier, inc=1, device_id={"blk": me + 2}, device_id_type=MESH)

    @pl.when(row > 0)
    def _():
        pl.semaphore_signal(barrier, inc=1, device_id={"blk": me - 2}, device_id_type=MESH)

    peers = 1 + (row < line - 1).astype(jnp.int32) + (row > 0).astype(jnp.int32)
    pl.semaphore_wait(barrier, peers)


def gather_kernel(
    blocks, x_ref, d_ref, xo_ref, do_ref, hold, own_sem, up_s, up_r, dn_s, dn_r, ac_s, ac_r, ex_s, ex_r
):
    me, line, row, col, partner = place(blocks)
    outs = (xo_ref, do_ref)
    ins = (x_ref, d_ref)
    above, below = me + 2, me - 2

    def up_copy(c, src, block, s):
        return remote(src, outs[c].at[block], up_s.at[c, s], up_r.at[c, s], above)

    def dn_copy(c, src, block, s):
        return remote(src, outs[c].at[block], dn_s.at[c, s], dn_r.at[c, s], below)

    def ac_copy(c, src, at):
        return remote(
            src, outs[c].at[2 * at + col], ac_s.at[c, at], ac_r.at[c, at], partner
        )

    def ac_arrival(c, at):
        ref = outs[c].at[2 * at + 1 - col]
        return remote(ref, ref, ac_s.at[c, at], ac_r.at[c, at], partner)

    def ex_copy(direction, to):
        ref = do_ref.at[partner]
        return remote(ref, ref, ex_s.at[direction], ex_r.at[direction], to)

    def ex_arrival(direction, block, to):
        ref = do_ref.at[block]
        return remote(ref, ref, ex_s.at[direction], ex_r.at[direction], to)

    greet(me, line, row, partner)
    own = []
    for c in range(2):
        ac_copy(c, ins[c], row).start()

        @pl.when(row < line - 1)
        def _():
            up_copy(c, ins[c], me, 0).start()

        @pl.when(row > 0)
        def _():
            dn_copy(c, ins[c], me, 0).start()

    loads = []
    for c in range(2):
        copy = pltpu.make_async_copy(ins[c], hold.at[c], own_sem.at[0, c])
        copy.start()
        loads.append(copy)
    for c in range(2):
        loads[c].wait()
        copy = pltpu.make_async_copy(hold.at[c], outs[c].at[me], own_sem.at[1, c])
        copy.start()
        own.append(copy)
    for s in range(1, line):
        for c in range(2):

            @pl.when(row >= s)
            def _():
                block = me - 2 * s
                ref = outs[c].at[block]
                up_copy(c, ref, block, s - 1).wait_recv()
                if s < line - 1:

                    @pl.when(row < line - 1)
                    def _():
                        up_copy(c, ref, block, s).start()

                if c == 0 or s > 1:
                    ac_copy(c, ref, row - s).start()

            @pl.when(row + s < line)
            def _():
                block = me + 2 * s
                ref = outs[c].at[block]
                dn_copy(c, ref, block, s - 1).wait_recv()
                if s < line - 1:

                    @pl.when(row > 0)
                    def _():
                        dn_copy(c, ref, block, s).start()

                if c == 0 or s > 1:
                    ac_copy(c, ref, row + s).start()

        if s == 1:
            ac_arrival(1, row).wait_recv()

            @pl.when(row < line - 1)
            def _():
                ex_copy(0, above).start()

            @pl.when(row > 0)
            def _():
                ex_copy(1, below).start()

    ac_arrival(0, row).wait_recv()
    ac_copy(0, x_ref, row).wait_send()
    ac_copy(1, d_ref, row).wait_send()
    for s in range(1, line):
        for c in range(2):
            for ok, at in ((row >= s, row - s), (row + s < line, row + s)):

                @pl.when(ok)
                def _():
                    if c == 0 or s > 1:
                        ac_arrival(c, at).wait_recv()
                        ac_copy(c, outs[c].at[2 * at + col], at).wait_send()

    @pl.when(row > 0)
    def _():
        ex_arrival(0, partner - 2, above).wait_recv()
        ex_copy(1, below).wait_send()

    @pl.when(row < line - 1)
    def _():
        ex_arrival(1, partner + 2, below).wait_recv()
        ex_copy(0, above).wait_send()

    for s in range(line - 1):
        for c in range(2):

            @pl.when((row >= s) & (row < line - 1))
            def _():
                src = ins[c] if s == 0 else outs[c].at[me - 2 * s]
                up_copy(c, src, me - 2 * s, s).wait_send()

            @pl.when((row + s < line) & (row > 0))
            def _():
                src = ins[c] if s == 0 else outs[c].at[me + 2 * s]
                dn_copy(c, src, me + 2 * s, s).wait_send()

    for copy in own:
        copy.wait()


def gather_rows(blocks, x, dy):
    line = blocks // 2
    shape = jax.ShapeDtypeStruct((blocks,) + x.shape, x.dtype)
    dma = pltpu.SemaphoreType.DMA
    got = pl.pallas_call(
        functools.partial(gather_kernel, blocks),
        out_shape=(shape, shape),
        in_specs=[pl.BlockSpec(memory_space=pl.ANY)] * 2,
        out_specs=(pl.BlockSpec(memory_space=pl.ANY),) * 2,
        scratch_shapes=[pltpu.VMEM((2,) + x.shape, x.dtype), dma((2, 2))] + [dma((2, line))] * 6 + [dma((2,))] * 2,
        compiler_params=pltpu.CompilerParams(
            collective_id=0, has_side_effects=True, vmem_limit_bytes=vmem_grant
        ),
        name="gather_rows",
    )(x, dy)
    return [part.reshape((-1,) + x.shape[1:]) for part in got]


def scatter_kernel(
    blocks,
    m_ref,
    b_ref,
    mo_ref,
    bo_ref,
    pair_buf,
    line_buf,
    top_buf,
    ex_buf,
    cross_buf,
    ac_s,
    ac_r,
    up_s,
    up_r,
    dn_s,
    dn_r,
    ex_s,
    ex_r,
):
    me, line, row, col, partner = place(blocks)
    parts = (m_ref, b_ref)
    outs = (mo_ref, bo_ref)
    above, below = me + 2, me - 2
    width = m_ref.shape[-1]
    tile = width // 8

    def total(dst, srcs):
        def body(k, carry):
            at = pl.ds(pl.multiple_of(k * tile, tile), tile)
            acc = srcs[0][:, at].astype(f32)
            for src in srcs[1:]:
                acc = acc + src[:, at].astype(f32)
            dst[:, at] = acc.astype(dst.dtype)
            return carry

        lax.fori_loop(0, width // tile, body, 0)

    def ac_copy(c, src, at):
        return remote(src, pair_buf.at[c, at], ac_s.at[c, at], ac_r.at[c, at], partner)

    def up_copy(c, at):
        return remote(
            pair_buf.at[c, at], line_buf.at[c, at], up_s.at[c, at], up_r.at[c, at], above
        )

    def dn_copy(c, at, landing):
        return remote(pair_buf.at[c, at], landing, dn_s.at[c, at], dn_r.at[c, at], below)

    def ex_copy(direction, block, to):
        return remote(
            b_ref.at[block], ex_buf.at[direction], ex_s.at[direction], ex_r.at[direction], to
        )

    greet(me, line, row, partner)

    @pl.when(row < line - 1)
    def _():
        ex_copy(0, partner + 2, above).start()

    @pl.when(row > 0)
    def _():
        ex_copy(1, partner - 2, below).start()

    def spots(s):
        if s == 0:
            return ((None, row),)
        return ((row + s < line, row + s), (row >= s, row - s))

    def crossing(c, s):
        return c == 0 or s > 1

    def guard(ok, body):
        if ok is None:
            body()
        else:
            pl.when(ok)(body)

    for s in range(line - 1, -1, -1):
        for c in range(2):
            for ok, at in spots(s):
                if crossing(c, s):
                    guard(ok, lambda: ac_copy(c, parts[c].at[2 * at + 1 - col], at).start())

    @pl.when(row > 0)
    def _():
        ex_copy(0, partner, above).wait_recv()

    @pl.when(row < line - 1)
    def _():
        ex_copy(1, partner, below).wait_recv()

    @pl.when((row > 0) & (row < line - 1))
    def _():
        total(cross_buf, (b_ref.at[partner], ex_buf.at[0], ex_buf.at[1]))

    @pl.when(row == 0)
    def _():
        total(cross_buf, (b_ref.at[partner], ex_buf.at[1]))

    @pl.when((row > 0) & (row == line - 1))
    def _():
        total(cross_buf, (b_ref.at[partner], ex_buf.at[0]))

    ac_copy(1, cross_buf, row).start()

    for s in range(line - 1, 0, -1):
        for c in range(2):

            @pl.when(row + s < line)
            def _():
                at = row + s
                slot = pair_buf.at[c, at]
                mine = parts[c].at[2 * at + col]
                base = (mine,)
                if crossing(c, s):
                    ac_copy(c, mine, at).wait_recv()
                    base = (mine, slot)
                if s < line - 1:

                    @pl.when(row > 0)
                    def _():
                        up_copy(c, at).wait_recv()
                        total(slot, base + (line_buf.at[c, at],))

                @pl.when(row == 0)
                def _():
                    total(slot, base)

                up_copy(c, at).start()

            @pl.when(row >= s)
            def _():
                at = row - s
                slot = pair_buf.at[c, at]
                mine = parts[c].at[2 * at + col]
                base = (mine,)
                if crossing(c, s):
                    ac_copy(c, mine, at).wait_recv()
                    base = (mine, slot)
                if s < line - 1:

                    @pl.when(row < line - 1)
                    def _():
                        dn_copy(c, at, line_buf.at[c, at]).wait_recv()
                        total(slot, base + (line_buf.at[c, at],))

                @pl.when(row == line - 1)
                def _():
                    total(slot, base)

                if s == 1:
                    dn_copy(c, at, top_buf.at[c]).start()
                else:
                    dn_copy(c, at, line_buf.at[c, at]).start()

    for c in range(2):
        mine = parts[c].at[me]
        slot = pair_buf.at[c, row]
        from_below = line_buf.at[c, row]
        from_above = top_buf.at[c]
        ac_copy(c, mine, row).wait_recv()

        @pl.when(row > 0)
        def _():
            up_copy(c, row).wait_recv()

        @pl.when(row < line - 1)
        def _():
            dn_copy(c, row, from_above).wait_recv()

        @pl.when((row > 0) & (row < line - 1))
        def _():
            total(outs[c], (mine, slot, from_below, from_above))

        @pl.when(row == 0)
        def _():
            total(outs[c], (mine, slot, from_above))

        @pl.when((row > 0) & (row == line - 1))
        def _():
            total(outs[c], (mine, slot, from_below))

    ac_copy(0, m_ref.at[partner], row).wait_send()
    ac_copy(1, cross_buf, row).wait_send()
    for s in range(1, line):
        for c in range(2):
            for ok, at in spots(s):
                if crossing(c, s):
                    guard(ok, lambda: ac_copy(c, parts[c].at[2 * at + 1 - col], at).wait_send())

            @pl.when(row + s < line)
            def _():
                up_copy(c, row + s).wait_send()

            @pl.when(row >= s)
            def _():
                dn_copy(c, row - s, line_buf.at[c, row - s]).wait_send()

    @pl.when(row < line - 1)
    def _():
        ex_copy(0, partner + 2, above).wait_send()

    @pl.when(row > 0)
    def _():
        ex_copy(1, partner - 2, below).wait_send()


def scatter_rows(blocks, mixed_terms, back_terms):
    line = blocks // 2
    rows = mixed_terms.shape[0] // blocks
    width = mixed_terms.shape[1]
    dma = pltpu.SemaphoreType.DMA
    block = jax.ShapeDtypeStruct((rows, width), bf16)
    block_bytes = 2 * rows * width
    return pl.pallas_call(
        functools.partial(scatter_kernel, blocks),
        out_shape=(block, block),
        in_specs=[pl.BlockSpec(memory_space=pltpu.VMEM)] * 2,
        out_specs=(pl.BlockSpec(memory_space=pltpu.VMEM),) * 2,
        scratch_shapes=[
            pltpu.VMEM((2, line, rows, width), bf16),
            pltpu.VMEM((2, line, rows, width), bf16),
            pltpu.VMEM((2, rows, width), bf16),
            pltpu.VMEM((2, rows, width), bf16),
            pltpu.VMEM((rows, width), bf16),
        ]
        + [dma((2, line))] * 6
        + [dma((2,))] * 2,
        compiler_params=pltpu.CompilerParams(
            collective_id=3,
            has_side_effects=True,
            vmem_limit_bytes=block_bytes * (2 * blocks + 4 * line + 12) + 2 * 2**20,
        ),
        name="scatter_rows",
    )(
        mixed_terms.reshape(blocks, rows, width),
        back_terms.reshape(blocks, rows, width),
    )


def sum_kernel(blocks, c_ref, o_ref, land, send_sem, recv_sem):
    me = lax.axis_index("blk")
    barrier = pltpu.get_barrier_semaphore()
    for k in range(1, blocks):
        pl.semaphore_signal(
            barrier, inc=1, device_id={"blk": lax.rem(me + k, blocks)}, device_id_type=MESH
        )
    pl.semaphore_wait(barrier, blocks - 1)
    copies = []
    for k in range(1, blocks):
        copy = remote(
            c_ref, land.at[k], send_sem.at[k], recv_sem.at[k], lax.rem(me + k, blocks)
        )
        copy.start()
        copies.append(copy)
    acc = c_ref[...].astype(f32)
    for k in range(1, blocks):
        copies[k - 1].wait_recv()
        acc = acc + land[k].astype(f32)
    o_ref[...] = acc.astype(o_ref.dtype)
    for copy in copies:
        copy.wait_send()


def sum_over_blk(blocks, coeffs, collective_id):
    dma = pltpu.SemaphoreType.DMA
    return pl.pallas_call(
        functools.partial(sum_kernel, blocks),
        out_shape=jax.ShapeDtypeStruct(coeffs.shape, coeffs.dtype),
        in_specs=[pl.BlockSpec(memory_space=pltpu.VMEM)],
        out_specs=pl.BlockSpec(memory_space=pltpu.VMEM),
        scratch_shapes=[
            pltpu.VMEM((blocks,) + coeffs.shape, coeffs.dtype),
            dma((blocks,)),
            dma((blocks,)),
        ],
        compiler_params=pltpu.CompilerParams(
            collective_id=collective_id, has_side_effects=True, vmem_limit_bytes=8 * 2**20
        ),
        name="sum_over_blk",
    )(coeffs)


adapter_scale = 2.0


def silu_pair(gate_in):
    sigmoid_val = jax.nn.sigmoid(gate_in)
    return (gate_in * sigmoid_val, sigmoid_val * (1.0 + gate_in * (1.0 - sigmoid_val)))


def dot(a, b, dims=((1,), (0,))):
    return lax.dot_general(a, b, (dims, ((), ())), preferred_element_type=f32)


def ranks_pattern(rank, entries):
    column = lax.broadcasted_iota(jnp.int32, (rank, entries * rank), 1)
    row = lax.broadcasted_iota(jnp.int32, (rank, entries * rank), 0)
    return (column % rank == row).astype(bf16)


def lanes_entry(rank, first, count):
    return (lax.broadcasted_iota(jnp.int32, (1, count), 1) // rank) + first


def spread_kernel(coeffs, mask, pattern):
    return jnp.where(mask, dot(coeffs, pattern), 0.0).astype(bf16)


def select_kernel(full, mask, pattern):
    kept = jnp.where(mask, full, 0.0).astype(bf16)
    return dot(pattern, kept, ((1,), (1,)))


def inputs_kernel(
    rank, x, d, gw, uw, dw, ag, au, bd, slot, pat, gate_o, up_o, gh_o, low_o, qg, qu, qd
):
    step = pl.program_id(0)
    xv, dv = x[...], d[...]
    terms = (
        (gate_o, lambda: dot(xv, gw[...])),
        (up_o, lambda: dot(xv, uw[...])),
        (gh_o, lambda: dot(dv, dw[...], ((1,), (1,)))),
        (qg, lambda: dot(xv, ag[...], ((1,), (1,)))),
        (qu, lambda: dot(xv, au[...], ((1,), (1,)))),
        (qd, lambda: dot(dv, bd[...], ((1,), (1,)))),
    )

    @pl.when(step == 0)
    def _():
        for ref, _term in terms:
            ref[...] = jnp.zeros_like(ref)

    for ref, term in terms:
        ref[...] += term()

    @pl.when(step == pl.num_programs(0) - 1)
    def _():
        mask = slot[...] == lanes_entry(rank, 0, qg.shape[1])
        for k, (ref, scale) in enumerate(((qg, 1.0), (qu, 1.0), (qd, adapter_scale))):
            low_o[k * rank : (k + 1) * rank, :] = (
                scale * select_kernel(ref[...], mask, pat[...])
            ).astype(bf16)


def input_terms(rank, x, dy, gw, uw, dw, ag, au, bd, slot, pat):
    rows, width = x.shape
    units, own = gw.shape[1], ag.shape[0]
    tile = min(512, width)
    across = lambda n: pl.BlockSpec((n, tile), lambda i: (0, i))
    down = lambda n: pl.BlockSpec((tile, n), lambda i: (i, 0))
    whole = lambda *shape: pl.BlockSpec(shape, lambda i: (0, 0))
    acc = jax.ShapeDtypeStruct((rows, units), f32)
    return pl.pallas_call(
        functools.partial(inputs_kernel, rank),
        grid=(width // tile,),
        out_shape=(acc, acc, acc, jax.ShapeDtypeStruct((3 * rank, rows), bf16)),
        in_specs=[
            across(rows),
            across(rows),
            down(units),
            down(units),
            across(units),
            across(own),
            across(own),
            across(own),
            whole(rows, 1),
            whole(*pat.shape),
        ],
        out_specs=(whole(rows, units),) * 3 + (whole(3 * rank, rows),),
        scratch_shapes=[pltpu.VMEM((rows, own), f32)] * 3,
        compiler_params=pltpu.CompilerParams(vmem_limit_bytes=vmem_grant),
        cost_estimate=pl.CostEstimate(
            flops=6 * rows * width * (units + own),
            bytes_accessed=6 * width * (units + own),
            transcendentals=0,
        ),
        name="input_terms",
    )(x, dy, gw, uw, dw, ag, au, bd, slot, pat)


def middle_kernel(
    rank, gate, up, gh, coeffs, tenant, pat, bg, bu, ad, hid_o, gg_o, gu_o, low_o, sg, su, sh, low
):
    half, step = pl.program_id(0), pl.program_id(1)
    last = pl.num_programs(1) - 1
    count = bg.shape[0]
    mask = tenant[...] == lanes_entry(rank, step * (count // rank), count)

    @pl.when((half == 0) & (step == 0))
    def _():
        sg[...] = gate[...]
        su[...] = up[...]
        sh[...] = gh[...]

    @pl.when(half == 0)
    def _():
        for k, (acc, fac, scale) in enumerate(
            ((sg, bg, adapter_scale), (su, bu, adapter_scale), (sh, ad, 1.0))
        ):
            given = coeffs[:, k * rank : (k + 1) * rank]
            acc[...] += scale * dot(spread_kernel(given, mask, pat[...]), fac[...])

    @pl.when((half == 0) & (step == last))
    def _():
        act_val, act_slope = silu_pair(sg[...])
        up_val, grad_h = su[...], sh[...]
        hid_o[...] = (act_val * up_val).astype(bf16)
        gg_o[...] = (grad_h * up_val * act_slope).astype(bf16)
        gu_o[...] = (grad_h * act_val).astype(bf16)
        low[...] = jnp.zeros_like(low)

    @pl.when(half == 1)
    def _():
        for k, (rows, fac, scale) in enumerate(
            ((hid_o, ad, 1.0), (gg_o, bg, adapter_scale), (gu_o, bu, adapter_scale))
        ):
            full = dot(rows[...], fac[...], ((1,), (1,)))
            low[k * rank : (k + 1) * rank, :] += scale * select_kernel(full, mask, pat[...])

    @pl.when((half == 1) & (step == last))
    def _():
        low_o[...] = low[...].astype(bf16)


def middle_terms(rank, gate, up, gh, coeffs, tenant, bg, bu, ad):
    rows, units = gate.shape
    total = bg.shape[0]
    tile = min(1024, total)
    pat = ranks_pattern(rank, tile // rank)
    whole = lambda *shape: pl.BlockSpec(shape, lambda h, i: (0, 0))
    down = pl.BlockSpec((tile, units), lambda h, i: (i, 0))
    block = jax.ShapeDtypeStruct((rows, units), bf16)
    return pl.pallas_call(
        functools.partial(middle_kernel, rank),
        grid=(2, total // tile),
        out_shape=(block, block, block, jax.ShapeDtypeStruct((3 * rank, rows), bf16)),
        in_specs=[whole(rows, units)] * 3
        + [whole(rows, 3 * rank), whole(rows, 1), whole(*pat.shape)]
        + [down] * 3,
        out_specs=(whole(rows, units),) * 3 + (whole(3 * rank, rows),),
        scratch_shapes=[pltpu.VMEM((rows, units), f32)] * 3
        + [pltpu.VMEM((3 * rank, rows), f32)],
        compiler_params=pltpu.CompilerParams(vmem_limit_bytes=vmem_grant),
        cost_estimate=pl.CostEstimate(
            flops=12 * rows * total * units,
            bytes_accessed=12 * total * units,
            transcendentals=rows * units,
        ),
        name="middle_terms",
    )(gate, up, gh, coeffs, tenant, pat, bg, bu, ad)


def outputs_kernel(
    rank, hid, gg, gu, sums, slot, pat, gw, uw, dw, ag, au, bd, mixed_o, back_o, eq, eg, eu
):
    @pl.when(pl.program_id(0) == 0)
    def _():
        mask = slot[...] == lanes_entry(rank, 0, eq.shape[1])
        for k, (ref, scale) in enumerate(((eq, adapter_scale), (eg, 1.0), (eu, 1.0))):
            given = sums[:, k * rank : (k + 1) * rank]
            ref[...] = (
                scale * jnp.where(mask, dot(given, pat[...]), 0.0)
            ).astype(bf16)

    mixed_o[...] = (dot(hid[...], dw[...]) + dot(eq[...], bd[...])).astype(bf16)
    back_o[...] = (
        dot(gg[...], gw[...], ((1,), (1,)))
        + dot(gu[...], uw[...], ((1,), (1,)))
        + dot(eg[...], ag[...])
        + dot(eu[...], au[...])
    ).astype(bf16)


def output_terms(rank, hid, gg, gu, sums, slot, pat, gw, uw, dw, ag, au, bd):
    rows, units = hid.shape
    width, own = ag.shape[1], ag.shape[0]
    tile = min(512, width)
    across = lambda n: pl.BlockSpec((n, tile), lambda i: (0, i))
    down = lambda n: pl.BlockSpec((tile, n), lambda i: (i, 0))
    whole = lambda *shape: pl.BlockSpec(shape, lambda i: (0, 0))
    block = jax.ShapeDtypeStruct((rows, width), bf16)
    return pl.pallas_call(
        functools.partial(outputs_kernel, rank),
        grid=(width // tile,),
        out_shape=(block, block),
        in_specs=[whole(rows, units)] * 3
        + [whole(rows, 3 * rank), whole(rows, 1), whole(*pat.shape)]
        + [down(units), down(units), across(units), across(own), across(own), across(own)],
        out_specs=(across(rows), across(rows)),
        scratch_shapes=[pltpu.VMEM((rows, own), bf16)] * 3,
        compiler_params=pltpu.CompilerParams(vmem_limit_bytes=vmem_grant),
        cost_estimate=pl.CostEstimate(
            flops=6 * rows * width * (units + own),
            bytes_accessed=6 * width * (units + own),
            transcendentals=0,
        ),
        name="output_terms",
    )(hid, gg, gu, sums, slot, pat, gw, uw, dw, ag, au, bd)


def grads_kernel(rank, coeffs, owner, pat, *refs):
    count = len(refs) // 3
    values, outs, weights = refs[:count], refs[count : 2 * count], refs[2 * count :]

    @pl.when(pl.program_id(1) == 0)
    def _():
        entries = pat.shape[0]
        line = lax.broadcasted_iota(jnp.int32, (entries, 1), 0) // rank
        mask = line + pl.program_id(0) * (entries // rank) == owner[...]
        for k, ref in enumerate(weights):
            given = coeffs[:, k * rank : (k + 1) * rank]
            ref[...] = jnp.where(mask, dot(pat[...], given, ((1,), (1,))), 0.0).astype(bf16)

    for value, out, weight in zip(values, outs, weights):
        out[...] = dot(weight[...], value[...])


def outer_sums(rank, entries, coeffs, owner, values, columns, name):
    rows, width = values[0][0].shape[0], columns
    tall = min(256, entries * rank)
    tile = min(1024, width)
    pat = jnp.transpose(ranks_pattern(rank, tall // rank))
    whole = lambda *shape: pl.BlockSpec(shape, lambda i, j: (0, 0))
    out = jax.ShapeDtypeStruct((entries * rank, width), f32)
    found = pl.pallas_call(
        functools.partial(grads_kernel, rank),
        grid=(entries * rank // tall, width // tile),
        out_shape=(out,) * len(values),
        in_specs=[whole(rows, coeffs.shape[1]), whole(1, rows), whole(*pat.shape)]
        + [
            pl.BlockSpec((rows, tile), lambda i, j, at=start // tile: (0, at + j))
            for _, start in values
        ],
        out_specs=(pl.BlockSpec((tall, tile), lambda i, j: (i, j)),) * len(values),
        scratch_shapes=[pltpu.VMEM((tall, rows), bf16)] * len(values),
        compiler_params=pltpu.CompilerParams(vmem_limit_bytes=vmem_grant),
        name=name,
    )(coeffs, owner, pat, *[value for value, _ in values])
    return [part.reshape(entries, rank, width) for part in found]


def local(
    tokens,
    cotangent,
    gate_weight,
    up_weight,
    down_weight,
    a_gate,
    a_up,
    down_output_factors,
    b_gate,
    b_up,
    a_down,
    tenant_of_row,
    adapter_slot,
):
    own_rows, width = tokens.shape
    blocks = lax.axis_size("blk")
    grp_count = lax.axis_size("grp")
    blk_index = lax.axis_index("blk")
    grp_index = lax.axis_index("grp")
    per_owner, rank = a_gate.shape[:2]
    tenant_count, _, units = b_gate.shape
    capacity = 2 * own_rows
    group_rows = own_rows * blocks
    x, dy = gather_rows(blocks, tokens, cotangent)

    layout = tenant_of_row.reshape(blocks, grp_count, own_rows)
    all_tenants = jnp.transpose(layout, (1, 0, 2)).reshape(grp_count, group_rows)
    tenant_hot = all_tenants[:, :, None] == jnp.arange(tenant_count, dtype=jnp.int32)
    all_slots = jnp.sum(jnp.where(tenant_hot, adapter_slot, 0), axis=2)
    mine = all_slots // per_owner == blk_index
    within = jnp.cumsum(mine.astype(jnp.int32), axis=1) - 1
    choose = mine[:, None, :] & (
        within[:, None, :] == jnp.arange(capacity, dtype=jnp.int32)[None, :, None]
    )
    choose_bf = choose.astype(bf16)
    picked_slot = (
        jnp.max(jnp.where(choose, all_slots[:, None, :], -1), axis=2).reshape(1, -1)
    )
    tenants = lax.dynamic_index_in_dim(all_tenants, grp_index, 0, keepdims=False)
    slots = lax.dynamic_index_in_dim(all_slots, grp_index, 0, keepdims=False)
    choose_own = lax.dynamic_index_in_dim(choose_bf, grp_index, 0, keepdims=False)

    local_slot = (slots - blk_index * per_owner)[:, None]
    slot_pattern = ranks_pattern(rank, per_owner)

    own_x = dot(choose_own, x).astype(bf16)
    own_dy = dot(choose_own, dy).astype(bf16)

    ag = a_gate.reshape(per_owner * rank, width)
    au = a_up.reshape(per_owner * rank, width)
    bd = down_output_factors.reshape(per_owner * rank, width)
    bg = b_gate.reshape(tenant_count * rank, units)
    bu = b_up.reshape(tenant_count * rank, units)
    ad = a_down.reshape(tenant_count * rank, units)

    gate_in, up_in, grad_in, low_in = input_terms(
        rank, x, dy, gate_weight, up_weight, down_weight, ag, au, bd, local_slot, slot_pattern
    )
    low_in, own_x, own_dy = lax.optimization_barrier((low_in, own_x, own_dy))
    all_x = lax.all_gather(own_x, "grp", axis=0, tiled=True)
    all_dy = lax.all_gather(own_dy, "grp", axis=0, tiled=True)
    twice = jnp.asarray(adapter_scale, bf16)
    coeffs = jnp.transpose(sum_over_blk(blocks, low_in, 1))
    hidden, grad_gate, grad_up, low_out = middle_terms(
        rank, gate_in, up_in, grad_in, coeffs, tenants[:, None], bg, bu, ad
    )
    sums = jnp.transpose(sum_over_blk(blocks, low_out, 2))

    packed = jnp.concatenate((hidden, grad_gate, grad_up, coeffs, sums), axis=1)
    spare = -packed.shape[1] % 128
    packed = jnp.pad(packed, ((0, 0), (0, spare)))
    everyone = lax.all_gather(packed, "grp", axis=0, tiled=True)

    mixed_terms, back_terms = output_terms(
        rank,
        hidden,
        grad_gate,
        grad_up,
        sums,
        local_slot,
        slot_pattern,
        gate_weight,
        up_weight,
        down_weight,
        ag,
        au,
        bd,
    )
    mixed, input_grad = scatter_rows(blocks, mixed_terms, back_terms)

    all_small = everyone[:, 3 * units : 3 * units + 6 * rank]
    picked = jnp.einsum(
        "gcn,gnk->gck",
        choose_bf,
        all_small[:, 3 * rank :].reshape(grp_count, group_rows, 3 * rank),
        preferred_element_type=f32,
    ).astype(bf16)
    picked = picked.reshape(grp_count * capacity, 3 * rank)
    slots_dev = per_owner // grp_count
    first_slot = blk_index * per_owner + grp_index * slots_dev
    picked = jnp.concatenate((twice * picked[:, :rank], picked[:, rank:]), axis=1)
    grad_bd, grad_ag, grad_au = outer_sums(
        rank,
        slots_dev,
        picked,
        picked_slot - first_slot,
        ((all_dy, 0), (all_x, 0), (all_x, 0)),
        width,
        "slot_grads",
    )
    tenant_dev = tenant_count // grp_count
    given = jnp.concatenate(
        (twice * all_small[:, : 2 * rank], all_small[:, 2 * rank : 3 * rank]), axis=1
    )
    grad_bg, grad_bu, grad_ad = outer_sums(
        rank,
        tenant_dev,
        given,
        all_tenants.reshape(1, -1) - grp_index * tenant_dev,
        ((everyone, units), (everyone, 2 * units), (everyone, 0)),
        units,
        "tenant_grads",
    )
    return (mixed, input_grad, grad_ag, grad_au, grad_bd, grad_bg, grad_bu, grad_ad)


def solution(mesh):
    placed = (
        P(("blk", "grp"), None),
        P(("blk", "grp"), None),
        P(None, "blk"),
        P(None, "blk"),
        P("blk", None),
        P("blk", None, None),
        P("blk", None, None),
        P("blk", None, None),
        P(None, None, "blk"),
        P(None, None, "blk"),
        P(None, None, "blk"),
        P(),
        P(),
    )
    return jax.shard_map(
        local,
        mesh=mesh,
        in_specs=placed,
        out_specs=(
            P(("blk", "grp"), None),
            P(("blk", "grp"), None),
            P(("blk", "grp"), None, None),
            P(("blk", "grp"), None, None),
            P(("blk", "grp"), None, None),
            P("grp", None, "blk"),
            P("grp", None, "blk"),
            P("grp", None, "blk"),
        ),
        check_vma=False,
    )
```
